512 devices in a mesh: dp: 32 (over y, x), seq: 16 (over z, core).
Axes of the slice: x: 4, y: 8, z: 8, core: 2. Of those that a mesh axis runs over, the one named last changes fastest.
Arguments:
- token_input: bfloat16 [32, 2048, 4096], P('dp', 'seq')
- input_map: bfloat16 [32, 2048, 128], P('dp', 'seq'), may hold values from -6 to 6
- output_map: bfloat16 [32, 2048, 128], P('dp', 'seq'), may hold values from -6 to 6
- step_size: float32 [32, 2048, 64], P('dp', 'seq'), may hold values from 0.005 to 0.1
- forget: float32 [32, 2048, 64], P('dp', 'seq'), as said below
- skip_gain: float32 [64], replicated, may hold values from 0.5 to 2
- segments: int32 [32, 16, 128], P('dp', 'seq'), may hold values from 0 to 7, never falling along the last dimension, each value on 1 to 32 neighbouring positions
- yield_rank: int32 [32, 128], P('dp'), may hold values from 0 to 63
- pair_mask: int32 [32, 128, 128], P('dp', 'seq'), may hold values from 0 to 1, as said below
- comparator: bfloat16 [4096, 64], replicated, may hold values from -0.01171875 to 0.01171875
Outputs:
- list_loss: float32 [32], P('dp')
- pooled_grad: float32 [32, 128, 4096], P('dp', 'seq')
- weight_grad: float32 [4096, 64], P(('dp', 'seq'))
The draws below stay inside these ranges and needn't reach their ends.
Inputs may be any that keep to these rules, and one draw needn't show every extreme that they name: `segments`: within each block the numbers never fall and every number of 0 to 7 occurs. pair_mask[g, i, j] equals pair_mask[g, j, i], and pair_mask[g, i, i] is 0. `forget`: Positive.
All inputs are finite; a program needn't handle non-finite values.
Results may differ from the reference program's by a relative error of at most 0.011.
Values may be sent and summed in bfloat16 or wider, within the bound.
A program may use at most 128 MiB of HBM per device.

```python
import math
import jax
import jax.numpy as jnp
import numpy as np
from jax import lax

H = 64
P_SIZE = 64
N = 128
L_DEV = 128
K_DEV = 8
LIST_TOTAL = 32
LIST_POSITIONS = 2048
CAND = 128
N_SEQ = 16


def draw_token_input(key, part):
    key_sequence = jax.random.split(key, 3)
    row_scale = jnp.exp(jax.random.uniform(key_sequence[1], (LIST_TOTAL, LIST_POSITIONS, 1), jnp.float32) * math.log(10.0))
    column_scale = jnp.exp(jax.random.uniform(key_sequence[2], (1, 1, H * P_SIZE), jnp.float32) * math.log(10.0))
    base_value = jax.random.normal(key_sequence[0], (LIST_TOTAL, LIST_POSITIONS, H * P_SIZE), jnp.float32)
    return (base_value * row_scale * column_scale * 0.1).astype(jnp.bfloat16)


def draw_forget(key, part):
    key_sequence = jax.random.split(key, 7)
    slow_heads = jax.random.randint(key_sequence[0], (H,), 0, 2) > 0
    slow_rate = 0.3 / LIST_POSITIONS * jnp.exp(jax.random.uniform(key_sequence[1], (H,), jnp.float32, -0.4, 0.4))
    fast_rate = jax.random.uniform(key_sequence[2], (H,), jnp.float32, 10.0, 16.0) / L_DEV
    base_rate = jnp.where(slow_heads, slow_rate, fast_rate)
    block_count = LIST_POSITIONS // L_DEV
    block_spread = jnp.exp(jax.random.uniform(key_sequence[3], (LIST_TOTAL, block_count, 1, H), jnp.float32, -0.45, 0.45))
    roughness = jax.random.uniform(key_sequence[4], (LIST_TOTAL, block_count, L_DEV, H), jnp.float32, 0.5, 2.0)
    decay_rate_value = (base_rate * block_spread * roughness).reshape(LIST_TOTAL, LIST_POSITIONS, H)
    spike_selection = jax.random.randint(key_sequence[5], (LIST_TOTAL, LIST_POSITIONS, 1), 0, LIST_POSITIONS) < 3
    spike_length = jax.random.uniform(key_sequence[6], (LIST_TOTAL, LIST_POSITIONS, 1), jnp.float32, 0.22, 0.69)
    return decay_rate_value + jnp.where(spike_selection, spike_length, 0.0)


def draw_pair_mask(key, part):
    picked = jax.random.randint(key, (LIST_TOTAL, CAND, CAND), 0, CAND * CAND)
    row_index = jax.lax.broadcasted_iota(jnp.int32, (CAND, CAND), 0)
    col_index = jax.lax.broadcasted_iota(jnp.int32, (CAND, CAND), 1)
    larger = jnp.maximum(row_index, col_index) + 1
    threshold = larger * larger
    mirrored = jnp.where(row_index < col_index, picked, jnp.swapaxes(picked, 1, 2))
    keep_pair = (mirrored < threshold) & (row_index != col_index)
    return keep_pair.astype(jnp.int32)


def set_ends(array, rng, least, high):
    extent = array.shape
    index_at = [jax.random.randint(jax.random.fold_in(rng, axis), (), 0, extent[axis]) for axis in range(len(extent))]
    array = array.at[tuple(index_at)].set(least)
    longest = extent.index(max(extent))
    index_at[longest] = (index_at[longest] + 1) % extent[longest]
    return array.at[tuple(index_at)].set(high)


def block_scale(own_key, dims, pieces, smallest, top_value):
    gain, own = 1.0, jax.random.fold_in(own_key, 6)
    for axis_at, parts in pieces:
        draws = jnp.exp(jax.random.uniform(jax.random.fold_in(own, axis_at), (parts,), jnp.float32, smallest / len(pieces), top_value / len(pieces)))
        gain = gain * jnp.repeat(draws, dims[axis_at] // parts).reshape([-1 if axis == axis_at else 1 for axis in range(len(dims))])
    return gain


def profile(count, total, reach, skew):
    loads = [(1 << 20) // math.isqrt(standing ** skew) + 1 for standing in range(2, count + 1)]
    surplus, counts = total - reach - (count - 1), [1] * (count - 1)
    while surplus > 0:
        free = [i for i in range(count - 1) if counts[i] < reach]
        mass, left = sum([loads[i] for i in free]), surplus
        for i in free:
            extra = min(reach - counts[i], max(1, left * loads[i] // mass), surplus)
            counts[i] = counts[i] + extra
            surplus = surplus - extra
    return np.array([reach] + counts)


def ragged_sizes(own_key, number_of, total, reach, lean):
    if number_of == 2:
        one = jax.random.randint(own_key, (), max(1, total - reach), min(reach, total - 1) + 1)
        return jnp.stack([one, total - one])
    tallies = jnp.asarray(profile(number_of, total, reach, lean), jnp.int32)
    pairs = (number_of - 1) // 2
    giver, sink = tallies[1:1 + 2 * pairs:2], tallies[2:2 + 2 * pairs:2]
    room = jnp.minimum(giver - 1, reach - sink)
    moved = jax.random.randint(jax.random.fold_in(own_key, 1), (pairs,), 0, 1 << 20) % (room + 1)
    tallies = tallies.at[1:1 + 2 * pairs:2].set(giver - moved).at[2:2 + 2 * pairs:2].set(sink + moved)
    return tallies[jax.random.permutation(jax.random.fold_in(own_key, 2), number_of)]


def bell_draw(own_key, extent, scale, bound, shards=(), kind=jnp.bfloat16):
    result = jax.random.normal(own_key, extent, jnp.float32) * scale
    if len(shards) > 0:
        result = block_scale(own_key, extent, shards, -0.22, 0.18) * result
    return jnp.clip(result, min=-bound, max=bound).astype(kind)


def setup_inputs(seed: int = 0) -> dict:
    arg_keys = jax.random.split(jax.random.key(seed), 11)
    token_input = draw_token_input(jax.random.fold_in(arg_keys[10], 71), 0)
    input_map = bell_draw(arg_keys[1], (LIST_TOTAL, LIST_POSITIONS, N), 1.0, 6.0, ((0, 32), (1, 16)))
    output_map = bell_draw(arg_keys[2], (LIST_TOTAL, LIST_POSITIONS, N), 1.0, 6.0, ((0, 32), (1, 16)))
    step_size = jnp.clip(jnp.exp(math.log(0.1) - 2.9957323 * jax.random.uniform(arg_keys[3], (LIST_TOTAL, LIST_POSITIONS, H), jnp.float32) ** block_scale(arg_keys[3], (LIST_TOTAL, LIST_POSITIONS, H), ((0, 32), (1, 16)), -0.2, 0.2)), 0.005, 0.1)
    forget = draw_forget(jax.random.fold_in(arg_keys[10], 71), 0)
    skip_gain = jnp.clip(jnp.exp(jax.random.uniform(arg_keys[5], (H,), jnp.float32, math.log(0.5), math.log(2.0))), 0.5, 2.0)
    segments = jax.vmap(lambda own: jnp.searchsorted(jnp.cumsum(ragged_sizes(own, K_DEV, L_DEV, 2 * L_DEV // K_DEV, 0)), jnp.arange(L_DEV), side="right"))(jax.random.split(arg_keys[6], LIST_TOTAL * N_SEQ)).reshape((LIST_TOTAL, N_SEQ, L_DEV)).astype(jnp.int32)
    yield_rank = set_ends(jax.random.randint(arg_keys[7], (LIST_TOTAL, CAND), 0, CAND // 2), jax.random.fold_in(arg_keys[7], 1), 0, (CAND // 2) - 1).astype(jnp.int32)
    pair_mask = draw_pair_mask(jax.random.fold_in(arg_keys[10], 71), 0)
    comparator = bell_draw(arg_keys[9], (H * P_SIZE, P_SIZE), (H * P_SIZE * P_SIZE) ** -0.5, 0.01171875)
    return {"token_input": token_input, "input_map": input_map, "output_map": output_map, "step_size": step_size, "forget": forget, "skip_gain": skip_gain, "segments": segments, "yield_rank": yield_rank, "pair_mask": pair_mask, "comparator": comparator}


full_precision = lax.Precision.HIGHEST
norm_epsilon = 1e-05

def block_scan(token_input, input_map, output_map, step_size, forget, skip_gain, carried):
    length, inner_width = token_input.shape
    head_count = step_size.shape[1]
    head_width = inner_width // head_count
    decay_log = jnp.cumsum(-forget, axis=0)
    block_total = decay_log[-1]
    scores = jnp.dot(output_map, input_map.T, preferred_element_type=jnp.float32)
    position = jnp.arange(length, dtype=jnp.int32)
    causal = position[:, None] >= position[None, :]
    group_outputs = []
    for group_index in range(head_count // 8):
        first_head = group_index * 8
        decay_part = decay_log[:, first_head:first_head + 8].T
        step_part = step_size[:, first_head:first_head + 8].T
        spacing = jnp.where(causal[None], decay_part[:, :, None] - decay_part[:, None, :], -jnp.inf)
        mixing = (scores[None] * jnp.exp(spacing) * step_part[:, None, :]).astype(jnp.bfloat16)
        group_values = token_input[:, first_head * head_width:(first_head + 8) * head_width].reshape(length, 8, head_width)
        group_outputs.append(jnp.einsum('gts,sgp->tgp', mixing.astype(jnp.float32), group_values.astype(jnp.float32)))
    local_out = jnp.concatenate(group_outputs, axis=1)
    token_heads = token_input.reshape(length, head_count, head_width)
    end_weight = jnp.exp(block_total[None, :] - decay_log) * step_size
    scaled = (token_heads * end_weight[:, :, None]).astype(jnp.bfloat16).reshape(length, inner_width)
    block_state = jnp.dot(scaled.T, input_map, preferred_element_type=jnp.float32).reshape(head_count, head_width, -1)
    carried_low = carried.astype(jnp.bfloat16).reshape(inner_width, -1)
    from_past = jnp.dot(output_map, carried_low.T, preferred_element_type=jnp.float32).reshape(length, head_count, head_width)
    layer_output = local_out + from_past * jnp.exp(decay_log)[:, :, None] + skip_gain[None, :, None] * token_heads
    new_state = jnp.exp(block_total)[:, None, None] * carried + block_state
    return (layer_output, new_state)

def pool_rows(layer_output, labels, nearby_candidate):
    length, head_count, head_width = layer_output.shape
    membership = (labels[None, :] == jnp.arange(nearby_candidate, dtype=jnp.int32)[:, None]).astype(jnp.float32)
    segment_sums = jnp.dot(membership, layer_output.reshape(length, head_count * head_width), precision=full_precision)
    segment_counts = lax.optimization_barrier(jnp.sum(membership, axis=1))
    segment_means = (segment_sums / segment_counts[:, None]).reshape(nearby_candidate, head_count, head_width)
    normalized = segment_means / jnp.sqrt(lax.optimization_barrier(jnp.mean(segment_means * segment_means, axis=2, keepdims=True)) + norm_epsilon)
    return normalized.reshape(nearby_candidate, head_count * head_width).astype(jnp.bfloat16)

def reference(token_input, input_map, output_map, step_size, forget, skip_gain, segments, yield_rank, pair_mask, comparator):
    list_count, length_all, inner_width = token_input.shape
    head_count = step_size.shape[2]
    head_width = inner_width // head_count
    state_width = input_map.shape[2]
    block_count = segments.shape[1]
    cand_count = block_count * K_DEV

    def one_list(packed):
        tok_list, in_list, out_list, step_list, forget_list, seg_list = packed

        def one_block(carried, block_data):
            tok_blk, in_blk, out_blk, step_blk, forget_blk, seg_blk = block_data
            layer_output, new_state = block_scan(tok_blk, in_blk, out_blk, step_blk, forget_blk, skip_gain, carried)
            return (new_state, pool_rows(layer_output, seg_blk, K_DEV))
        zero_state = jnp.zeros((head_count, head_width, state_width), jnp.float32)
        block_split = (tok_list.reshape(block_count, L_DEV, inner_width), in_list.reshape(block_count, L_DEV, state_width), out_list.reshape(block_count, L_DEV, state_width), step_list.reshape(block_count, L_DEV, head_count), forget_list.reshape(block_count, L_DEV, head_count), seg_list)
        _, pooled = lax.scan(one_block, zero_state, block_split)
        return pooled.reshape(cand_count, inner_width)
    pooled_all = lax.map(one_list, (token_input, input_map, output_map, step_size, forget, segments))
    head_weight = comparator.reshape(head_count, head_width, head_width)
    skewed = (jnp.swapaxes(head_weight, 1, 2).astype(jnp.float32) - head_weight.astype(jnp.float32)).astype(jnp.bfloat16)

    def compare(packed):
        pooled, rank_row, mask_rows = packed
        pooled_heads = pooled.reshape(cand_count, head_count, head_width).astype(jnp.float32)
        projected = jnp.einsum('cha,hab->chb', pooled_heads, head_weight.astype(jnp.float32)).astype(jnp.bfloat16)
        score = jnp.dot(projected.reshape(cand_count, inner_width), pooled.T, preferred_element_type=jnp.float32)
        margin = score - score.T
        target = jnp.where(rank_row[:, None] < rank_row[None, :], 1.0, jnp.where(rank_row[:, None] > rank_row[None, :], 0.0, 0.5)).astype(jnp.float32)
        valid_pairs = mask_rows.astype(jnp.float32)
        pair_loss = jnp.sum(valid_pairs * (jax.nn.softplus(margin) - target * margin)) / (cand_count * cand_count)
        pair_grad = (2.0 * valid_pairs * (jax.nn.sigmoid(margin) - target)).astype(jnp.bfloat16)
        skew_rows = jnp.einsum('cha,hab->chb', pooled_heads, skewed.astype(jnp.float32)).astype(jnp.bfloat16)
        pooled_grad = jnp.dot(pair_grad, skew_rows.reshape(cand_count, inner_width), preferred_element_type=jnp.float32)
        accumulated = jnp.dot(pair_grad, pooled, preferred_element_type=jnp.float32).reshape(cand_count, head_count, head_width)
        weight_part = jnp.einsum('cha,chb->hab', pooled_heads, accumulated, precision=full_precision)
        return (pair_loss, pooled_grad, weight_part)
    list_loss, pooled_grad, weight_parts = lax.map(compare, (pooled_all, yield_rank, pair_mask))
    weight_grad = (lax.optimization_barrier(jnp.sum(weight_parts, axis=0)) / (cand_count * list_count)).reshape(inner_width, head_width)
    return (list_loss, pooled_grad, weight_grad)
```

```python
import jax
import jax.numpy as jnp
from jax import lax
from jax.experimental import pallas as pl
from jax.experimental.pallas import tpu as pltpu
from jax.sharding import PartitionSpec as P

HI = lax.Precision.HIGHEST
F32 = jnp.float32
BF16 = jnp.bfloat16
EPS = 1e-05
NS = 16
ND = 32
MESH = pl.DeviceIdType.MESH


def dot(a, b, precision=None):
    return lax.dot_general(
        a, b, (((1,), (0,)), ((), ())), precision=precision, preferred_element_type=F32
    )


def dot_t(a, b):
    return lax.dot_general(a, b, (((1,), (1,)), ((), ())), preferred_element_type=F32)


def iota(shape, axis):
    return lax.broadcasted_iota(jnp.int32, shape, axis)


def block_kernel(
    skip, tok, b_in, c_out, step, forget, seg, st_o, v_o, m_o, d_o, cols, dl_rows, step_rows
):
    lower = iota((128, 128), 0) >= iota((128, 128), 1)
    dl = -dot(lower.astype(F32), forget[...], HI)
    end_weight = jnp.exp(dl[127:128, :] - dl) * step[...]
    cols[...] = jnp.concatenate([dl, end_weight], axis=1)
    dl_rows[...] = jnp.transpose(dl)
    step_rows[...] = jnp.transpose(step[...])
    b_t = jnp.transpose(b_in[...].astype(F32)).astype(BF16)
    scores = jnp.where(lower, dot_t(c_out[...], b_in[...]), 0.0)
    member = (jnp.broadcast_to(seg[...], (8, 128)) == iota((8, 128), 0)).astype(F32)
    member_low = member.astype(BF16)
    inverse = 1.0 / jnp.sum(member, axis=1, keepdims=True)
    left = iota((128, 128), 1) < 64
    left8 = left[:8]
    left1 = left[:1]

    def group(j, _):
        query_rows = []
        totals = []
        for pair in range(2):
            lanes = pl.ds(pl.multiple_of(j * 256 + pair * 128, 128), 128)
            tokens = tok[:, lanes]
            mixed = []
            for i in range(2):
                at = pair * 2 + i
                row = dl_rows[pl.ds(j * 4 + at, 1), :]
                gap = cols[:, at : at + 1] - row
                mixing = scores * jnp.exp(jnp.minimum(gap, 0.0)) * step_rows[pl.ds(j * 4 + at, 1), :]
                mixed.append(dot(member_low, mixing.astype(BF16)) + skip[j * 4 + at] * member)
                past = jnp.exp(row)
                query_rows.append(member * inverse * past)
                totals.append(past[:, 127:128])
            both = dot(jnp.concatenate(mixed, axis=0).astype(BF16), tokens)
            m_o[j, :, pair * 128 : pair * 128 + 128] = (
                jnp.where(left8, both[:8], both[8:]) * inverse
            )
            base = 64 + pair * 2
            weight = jnp.where(left, cols[:, base : base + 1], cols[:, base + 1 : base + 2])
            scaled = (tokens.astype(F32) * weight).astype(BF16)
            st_o[j, :, pair * 128 : pair * 128 + 128] = dot(b_t, scaled).astype(BF16)
        v_o[j] = dot(jnp.concatenate(query_rows, axis=0).astype(BF16), c_out[...]).astype(BF16)
        first = jnp.where(left1, totals[0], totals[1])
        second = jnp.where(left1, totals[2], totals[3])
        d_o[j] = jnp.where(iota((8, 128), 0) == 0, first, second)
        cols[...] = pltpu.roll(cols[...], 124, 1)
        return 0

    lax.fori_loop(0, 16, group, 0)


def list_kernel(
    st, v, m, d, w_in, rank, mask,
    pg_o, loss_o, wg_o,
    r_st, r_v, r_m, r_d, carried, means, margin_part, r_margin, pair_own, r_pair, grad_part, r_grad,
    w_part, r_w,
    send_a, recv_a, own_a, send_b, recv_b, send_c, recv_c, send_d, recv_d, send_w, recv_w,
):
    me_d = lax.axis_index("dp")
    me = lax.axis_index("seq")
    home = me_d // 2

    def peer(k):
        return lax.rem(me + k, NS)

    barrier = pltpu.get_barrier_semaphore()

    def greet(k, _):
        pl.semaphore_signal(barrier, inc=1, device_id=(me_d, peer(k)), device_id_type=MESH)
        return 0

    lax.fori_loop(1, NS, greet, 0)

    def greet_source(s, _):
        @pl.when(jnp.logical_or(s != me_d, home != me))
        def _():
            pl.semaphore_signal(barrier, inc=1, device_id=(s, home), device_id_type=MESH)

        return 0

    lax.fori_loop(0, ND, greet_source, 0)
    pl.semaphore_wait(barrier, NS - 1 + ND - (home == me).astype(jnp.int32))

    def exchange(src, dst, send, recv, k):
        return pltpu.make_async_remote_copy(
            src_ref=src, dst_ref=dst, send_sem=send, recv_sem=recv,
            device_id=(me_d, peer(k)), device_id_type=MESH,
        )

    arrays = ((st, r_st), (v, r_v), (m, r_m), (d, r_d))

    def copies(k):
        return [
            exchange(src.at[peer(k)], dst.at[me], send_a.at[n, k], recv_a.at[n, k], k)
            for n, (src, dst) in enumerate(arrays)
        ]

    def start_a(k, _):
        for c in copies(k):
            c.start()
        return 0

    lax.fori_loop(1, NS, start_a, 0)
    own = [
        pltpu.make_async_copy(src.at[me], dst.at[me], own_a.at[n])
        for n, (src, dst) in enumerate(arrays)
    ]
    for c in own:
        c.start()
    wide = w_in[...].astype(F32)
    same = (iota((256, 256), 0) // 64) == (iota((256, 256), 1) // 64)
    blocks = jnp.where(same, jnp.concatenate([wide, wide, wide, wide], axis=1), 0.0)
    weight = blocks.astype(BF16)
    skewed = (jnp.transpose(blocks) - blocks).astype(BF16)
    for c in own:
        c.wait()

    def wait_a(k, _):
        for c in copies(k):
            c.wait()
        return 0

    lax.fori_loop(1, NS, wait_a, 0)

    carried[...] = jnp.zeros_like(carried)
    lane = iota((8, 256), 1) // 64

    def block(b, _):
        now = carried[...]
        past = dot(r_v[b], now.astype(BF16))
        total = r_m[b]
        for h in range(4):
            total = total + jnp.where(lane == h, past[h * 8 : h * 8 + 8], 0.0)
        means[pl.ds(pl.multiple_of(b * 8, 8), 8), :] = total
        decay = jnp.concatenate([r_d[b, 0:1, :], r_d[b, 1:2, :]], axis=1)
        carried[...] = decay * now + r_st[b].astype(F32)
        return 0

    lax.fori_loop(0, NS, block, 0)
    mean = means[...]
    square = dot(mean * mean, jnp.where(same, 1.0 / 64.0, 0.0), HI)
    pooled32 = mean / jnp.sqrt(square + EPS)
    pooled = pooled32.astype(BF16)
    projected = dot(pooled, weight).astype(BF16)
    margin_part[...] = dot_t(projected, pooled) - dot_t(pooled, projected)

    def margin_copy(k):
        rows = pl.ds(pl.multiple_of(peer(k) * 8, 8), 8)
        return exchange(margin_part.at[rows], r_margin.at[k], send_b.at[k], recv_b.at[k], k)

    def start_b(k, _):
        margin_copy(k).start()
        return 0

    lax.fori_loop(1, NS, start_b, 0)
    r_margin[0] = margin_part[pl.ds(pl.multiple_of(me * 8, 8), 8), :]
    skew_rows = dot(pooled, skewed).astype(BF16)
    pooled_t = jnp.transpose(pooled.astype(F32))
    ranks = jnp.broadcast_to(rank[...].astype(F32), (8, 128))
    mine = iota((8, 128), 1) == me * 8 + iota((8, 128), 0)
    own_rank = jnp.sum(jnp.where(mine, ranks, 0.0), axis=1, keepdims=True)
    target = jnp.where(own_rank < ranks, 1.0, jnp.where(own_rank > ranks, 0.0, 0.5))
    valid = mask[...].astype(F32)

    def wait_b(k, _):
        margin_copy(k).wait()
        return 0

    lax.fori_loop(1, NS, wait_b, 0)
    margin = jnp.sum(r_margin[...], axis=0)
    soft = jnp.maximum(margin, 0.0) + jnp.log(1.0 + jnp.exp(-jnp.abs(margin)))
    losses = jnp.sum(valid * (soft - target * margin), axis=0, keepdims=True)
    pair = 2.0 * valid * (1.0 / (1.0 + jnp.exp(-margin)) - target)
    sent = jnp.concatenate([pair, jnp.broadcast_to(losses, (8, 128))], axis=0)
    pair_own[...] = sent
    r_pair[me] = sent

    def pair_copy(k):
        return exchange(pair_own, r_pair.at[me], send_c.at[k], recv_c.at[k], k)

    def start_c(k, _):
        pair_copy(k).start()
        return 0

    lax.fori_loop(1, NS, start_c, 0)

    def wait_c(k, _):
        pair_copy(k).wait()
        return 0

    lax.fori_loop(1, NS, wait_c, 0)
    pairs = r_pair[...]
    all_pair = pairs[:, :8, :].reshape(128, 128).astype(BF16)
    accumulated = dot(all_pair, pooled)
    product = dot(pooled_t, accumulated, HI) * (1.0 / 4096.0)
    for h in range(4):
        rows = slice(h * 64, h * 64 + 64)
        w_part[rows, 0:64] = product[rows, h * 64 : h * 64 + 64]

    def w_copy(i):
        to_d = me * 2 + i // NS
        to_s = lax.rem(i, NS)
        return to_d, to_s, pltpu.make_async_remote_copy(
            src_ref=w_part.at[pl.ds(pl.multiple_of(i * 8, 8), 8)],
            dst_ref=r_w.at[me_d],
            send_sem=send_w.at[i], recv_sem=recv_w.at[me_d],
            device_id=(to_d, to_s), device_id_type=MESH,
        )

    def start_w(i, _):
        to_d, to_s, c = w_copy(i)
        itself = jnp.logical_and(to_d == me_d, to_s == me)

        @pl.when(jnp.logical_not(itself))
        def _():
            c.start()

        @pl.when(itself)
        def _():
            r_w[me_d] = w_part[pl.ds(pl.multiple_of(i * 8, 8), 8), :]

        return 0

    w_part[:, 64:128] = jnp.zeros((256, 64), F32)
    lax.fori_loop(0, 2 * NS, start_w, 0)
    grad_part[...] = dot(all_pair, skew_rows)

    def grad_copy(k):
        rows = pl.ds(pl.multiple_of(peer(k) * 8, 8), 8)
        return exchange(grad_part.at[rows], r_grad.at[me], send_d.at[k], recv_d.at[k], k)

    def start_d(k, _):
        grad_copy(k).start()
        return 0

    lax.fori_loop(1, NS, start_d, 0)
    r_grad[me] = grad_part[pl.ds(pl.multiple_of(me * 8, 8), 8), :]
    loss = jnp.sum(pairs[:, 8, :]) * (1.0 / (128.0 * 128.0))
    loss_o[...] = jnp.full((8, 128), loss, F32)

    def wait_d(k, _):
        grad_copy(k).wait()
        return 0

    lax.fori_loop(1, NS, wait_d, 0)
    for b in range(NS):
        pg_o[:, b * 256 : b * 256 + 256] = r_grad[b]

    def wait_w(i, _):
        to_d, to_s, c = w_copy(i)

        @pl.when(jnp.logical_not(jnp.logical_and(to_d == me_d, to_s == me)))
        def _():
            c.wait_send()

        arrived = pltpu.make_async_remote_copy(
            src_ref=w_part.at[pl.ds(0, 8)], dst_ref=r_w.at[i],
            send_sem=send_w.at[i], recv_sem=recv_w.at[i],
            device_id=(to_d, to_s), device_id_type=MESH,
        )

        @pl.when(jnp.logical_or(i != me_d, home != me))
        def _():
            arrived.wait_recv()

        return 0

    lax.fori_loop(0, ND, wait_w, 0)
    wg_o[...] = jnp.sum(r_w[...], axis=0)[:, :64]


def per_device(
    token_input, input_map, output_map, step_size, forget, skip_gain, segments, yield_rank,
    pair_mask, comparator,
):
    vmem = pl.BlockSpec(memory_space=pltpu.VMEM)
    shape = jax.ShapeDtypeStruct
    st, v, m, d = pl.pallas_call(
        block_kernel,
        out_shape=(
            shape((16, 128, 256), BF16),
            shape((16, 32, 128), BF16),
            shape((16, 8, 256), F32),
            shape((16, 8, 128), F32),
        ),
        in_specs=[pl.BlockSpec(memory_space=pltpu.SMEM)] + [vmem] * 6,
        out_specs=(vmem,) * 4,
        scratch_shapes=[
            pltpu.VMEM((128, 128), F32),
            pltpu.VMEM((64, 128), F32),
            pltpu.VMEM((64, 128), F32),
        ],
        name="block",
    )(
        skip_gain, token_input[0], input_map[0], output_map[0], step_size[0], forget[0],
        segments[0],
    )
    own_weight = lax.dynamic_slice_in_dim(comparator, lax.axis_index("seq") * 256, 256)
    sem = pltpu.SemaphoreType.DMA
    pooled_grad, loss, weight_grad = pl.pallas_call(
        list_kernel,
        out_shape=(shape((8, 4096), F32), shape((8, 128), F32), shape((8, 64), F32)),
        in_specs=[vmem] * 7,
        out_specs=(vmem,) * 3,
        scratch_shapes=[
            pltpu.VMEM((16, 128, 256), BF16),
            pltpu.VMEM((16, 32, 128), BF16),
            pltpu.VMEM((16, 8, 256), F32),
            pltpu.VMEM((16, 8, 128), F32),
            pltpu.VMEM((128, 256), F32),
            pltpu.VMEM((128, 256), F32),
            pltpu.VMEM((128, 128), F32),
            pltpu.VMEM((16, 8, 128), F32),
            pltpu.VMEM((16, 128), F32),
            pltpu.VMEM((16, 16, 128), F32),
            pltpu.VMEM((128, 256), F32),
            pltpu.VMEM((16, 8, 256), F32),
            pltpu.VMEM((256, 128), F32),
            pltpu.VMEM((32, 8, 128), F32),
            sem((4, 16)), sem((4, 16)), sem((4,)),
            sem((16,)), sem((16,)), sem((16,)), sem((16,)), sem((16,)), sem((16,)),
            sem((32,)), sem((32,)),
        ],
        compiler_params=pltpu.CompilerParams(collective_id=0, has_side_effects=True),
        name="list",
    )(st, v, m, d, own_weight, yield_rank, pair_mask[0])
    return (loss[0, :1], pooled_grad[None], weight_grad)


def solution(mesh):
    return jax.shard_map(
        per_device,
        mesh=mesh,
        in_specs=(
            P("dp", "seq", None),
            P("dp", "seq", None),
            P("dp", "seq", None),
            P("dp", "seq", None),
            P("dp", "seq", None),
            P(),
            P("dp", "seq", None),
            P("dp", None),
            P("dp", "seq", None),
            P(),
        ),
        out_specs=(P("dp"), P("dp", "seq", None), P(("dp", "seq"), None)),
        check_vma=False,
    )
```

```python
import jax
import jax.numpy as jnp
from jax import lax
from jax.experimental import pallas as pl
from jax.experimental.pallas import tpu as pltpu
from jax.sharding import PartitionSpec as P

HI = lax.Precision.HIGHEST
F32 = jnp.float32
BF16 = jnp.bfloat16
EPS = 1e-05
NS = 16
ND = 32
CHIPS = 8
AHEAD = 4
MESH = pl.DeviceIdType.MESH


def dot(a, b, precision=None):
    return lax.dot_general(
        a, b, (((1,), (0,)), ((), ())), precision=precision, preferred_element_type=F32
    )


def dot_t(a, b):
    return lax.dot_general(a, b, (((1,), (1,)), ((), ())), preferred_element_type=F32)


def iota(shape, axis):
    return lax.broadcasted_iota(jnp.int32, shape, axis)


def list_kernel(
    skip, tok, b_in, c_out, step, forget, seg, w_in, rank, mask,
    pg_o, loss_o, wg_o,
    cols, dl_rows, give_s, give_m, own_s, own_m, got_s, got_m, pack, r_pack, w_own,
    carried, means, margin_part, r_margin, pair_own, r_pair, grad_part, r_grad, w_part, r_w,
    send_g, recv_g, send_m, recv_m, send_a, recv_a, send_b, recv_b, send_c, recv_c,
    send_d, recv_d, send_w, recv_w, w_sem,
):
    me_d = lax.axis_index("dp")
    me = lax.axis_index("seq")
    chip = me // 2
    core = lax.rem(me, 2)
    home = me_d // 2

    def peer(k):
        return lax.rem(me + k, NS)

    barrier = pltpu.get_barrier_semaphore()

    def greet_source(s, _):
        @pl.when(jnp.logical_or(s != me_d, home != me))
        def _():
            pl.semaphore_signal(barrier, inc=1, device_id=(s, home), device_id_type=MESH)

        return 0

    lax.fori_loop(0, ND, greet_source, 0)

    def greet(k, _):
        pl.semaphore_signal(barrier, inc=1, device_id=(me_d, peer(k)), device_id_type=MESH)
        return 0

    lax.fori_loop(1, NS, greet, 0)
    w_fetch = pltpu.make_async_copy(
        w_in.at[:, pl.ds(pl.multiple_of(me * 256, 256), 256)], w_own, w_sem
    )
    w_fetch.start()

    upper = iota((128, 128), 0) <= iota((128, 128), 1)
    lower = iota((128, 128), 0) >= iota((128, 128), 1)
    dl = -dot(forget[...], upper.astype(F32), HI)
    end_weight = jnp.exp(dl[:, 127:128] - dl) * step[...]
    dl_rows[...] = dl
    cols[...] = jnp.transpose(jnp.concatenate([dl, end_weight], axis=0))
    b_t = jnp.transpose(b_in[...].astype(F32)).astype(BF16)
    scores = jnp.where(lower, dot_t(c_out[...], b_in[...]), 0.0)
    member = (jnp.broadcast_to(seg[...], (8, 128)) == iota((8, 128), 0)).astype(F32)
    member_low = member.astype(BF16)
    inverse = 1.0 / jnp.sum(member, axis=1, keepdims=True)
    average = member * inverse
    left = iota((128, 128), 1) < 64
    left8 = left[:8]

    def group(j, out_s, out_m, t):
        here = pltpu.roll(cols[...], lax.rem(128 - 4 * j, 128), 1)
        query_rows = []
        for pair in range(2):
            lanes = pl.ds(pl.multiple_of(j * 256 + pair * 128, 128), 128)
            at_lanes = slice(pair * 128, pair * 128 + 128)
            tokens = tok[:, lanes]
            mixed = []
            totals = []
            for i in range(2):
                at = pair * 2 + i
                row = dl_rows[pl.ds(j * 4 + at, 1), :]
                gap = here[:, at : at + 1] - row
                mixing = scores * jnp.exp(jnp.minimum(gap, 0.0)) * step[pl.ds(j * 4 + at, 1), :]
                mixed.append(dot(member_low, mixing.astype(BF16)) + skip[j * 4 + at] * member)
                past = jnp.exp(row)
                query_rows.append(average * past)
                totals.append(past[:, 127:128])
            both = dot(jnp.concatenate(mixed, axis=0).astype(BF16), tokens)
            out_m[t, 0:8, at_lanes] = jnp.where(left8, both[:8], both[8:]) * inverse
            out_m[t, 8:16, at_lanes] = jnp.where(left8, totals[0], totals[1])
            base = 64 + pair * 2
            weight = jnp.where(left, here[:, base : base + 1], here[:, base + 1 : base + 2])
            scaled = (tokens.astype(F32) * weight).astype(BF16)
            out_s[t, 0:128, at_lanes] = dot(b_t, scaled).astype(BF16)
        queries = dot(jnp.concatenate(query_rows, axis=0).astype(BF16), c_out[...]).astype(BF16)
        out_s[t, 128:160, 0:128] = queries
        out_s[t, 128:160, 128:256] = queries

    def target_chip(t):
        away = CHIPS // 2 + (t // 2 + lax.rem(t, 2)) * (1 - 2 * lax.rem(t, 2))
        return lax.rem(chip + away, CHIPS)

    def compute(t, _):
        to = target_chip(t) * 2
        group(to + 1 - core, give_s, give_m, t)
        group(to + core, own_s, own_m, t)
        return 0

    def give(t):
        other = (me_d, chip * 2 + 1 - core)
        return (
            pltpu.make_async_remote_copy(
                src_ref=give_s.at[t], dst_ref=got_s.at[t], send_sem=send_g.at[t],
                recv_sem=recv_g.at[t], device_id=other, device_id_type=MESH,
            ),
            pltpu.make_async_remote_copy(
                src_ref=give_m.at[t], dst_ref=got_m.at[t], send_sem=send_m.at[t],
                recv_sem=recv_m.at[t], device_id=other, device_id_type=MESH,
            ),
        )

    def send_give(t, _):
        for c in give(t):
            c.start()
        return 0

    lane = iota((8, 256), 1) // 64

    def by_head(rows):
        total = jnp.where(lane == 0, rows[0:8], 0.0)
        for h in range(1, 4):
            total = total + jnp.where(lane == h, rows[h * 8 : h * 8 + 8], 0.0)
        return total

    def combine(t, out, at):
        for c in give(t):
            c.wait()
        first = core == 0
        mine, theirs = own_s[t], got_s[t]
        early = jnp.where(first, mine, theirs)
        late = jnp.where(first, theirs, mine)
        mine_m, theirs_m = own_m[t], got_m[t]
        early_m = jnp.where(first, mine_m, theirs_m)
        late_m = jnp.where(first, theirs_m, mine_m)
        early_d, late_d = early_m[8:9, :], late_m[8:9, :]
        state = late_d * early[:128].astype(F32) + late[:128].astype(F32)
        late_q = late[128:160, 0:128]
        within = by_head(dot(late_q, early[:128]))
        scaled_q = late_q.astype(F32)
        scaled_q = jnp.concatenate(
            [scaled_q[h * 8 : h * 8 + 8] * early_d[:, h * 64 : h * 64 + 1] for h in range(4)],
            axis=0,
        )
        out[at, 0:128, :] = state.astype(BF16)
        out[at, 128:160, 0:128] = early[128:160, 0:128]
        out[at, 128:160, 128:256] = scaled_q.astype(BF16)
        out[at, 160:176, :] = jnp.concatenate(
            [early_m[0:8], late_m[0:8] + within], axis=0
        ).astype(BF16)
        decay = early_d * late_d
        high = decay.astype(BF16).astype(F32)
        middle = (decay - high).astype(BF16).astype(F32)
        low = decay - high - middle
        which = iota((16, 256), 0)
        out[at, 176:192, :] = jnp.where(
            which == 0, high, jnp.where(which == 1, middle, low)
        ).astype(BF16)

    def package(t):
        return pltpu.make_async_remote_copy(
            src_ref=pack.at[t], dst_ref=r_pack.at[chip], send_sem=send_a.at[t],
            recv_sem=recv_a.at[t], device_id=(me_d, target_chip(t) * 2 + core),
            device_id_type=MESH,
        )

    lax.fori_loop(0, AHEAD, compute, 0)
    pl.semaphore_wait(barrier, NS - 1 + ND - (home == me).astype(jnp.int32))
    lax.fori_loop(0, AHEAD, send_give, 0)

    def middle(t, _):
        combine(t - AHEAD, pack, t - AHEAD)
        compute(t, 0)
        package(t - AHEAD).start()
        send_give(t, 0)
        return 0

    lax.fori_loop(AHEAD, CHIPS, middle, 0)
    combine(CHIPS - AHEAD, pack, CHIPS - AHEAD)

    def rest(t, _):
        combine(t, pack, t)
        package(t - 1).start()
        return 0

    lax.fori_loop(CHIPS - AHEAD + 1, CHIPS - 1, rest, 0)
    combine(CHIPS - 1, r_pack, chip)
    package(CHIPS - 2).start()

    w_fetch.wait()
    narrow = w_own[...].astype(F32)
    same = (iota((256, 256), 0) // 64) == (iota((256, 256), 1) // 64)
    blocks_t = jnp.where(same, jnp.concatenate([narrow, narrow, narrow, narrow], axis=0), 0.0)
    blocks = jnp.transpose(blocks_t)
    weight = blocks.astype(BF16)
    skewed = (blocks_t - blocks).astype(BF16)
    carried[...] = jnp.zeros_like(carried)

    def wait_a(t, _):
        package(t).wait()
        return 0

    lax.fori_loop(0, CHIPS - 1, wait_a, 0)

    def chip_step(b, _):
        now = carried[...]
        queries = jnp.concatenate([r_pack[b, 128:160, 0:128], r_pack[b, 128:160, 128:256]], axis=0)
        past = dot(queries, now.astype(BF16))
        local = r_pack[b, 160:176, :].astype(F32)
        means[pl.ds(pl.multiple_of(b * 16, 16), 16), :] = local + jnp.concatenate(
            [by_head(past[:32]), by_head(past[32:])], axis=0
        )
        parts = r_pack[b, 176:192, :].astype(F32)
        decay = parts[0:1] + (parts[1:2] + parts[2:3])
        carried[...] = decay * now + r_pack[b, 0:128, :].astype(F32)
        return 0

    lax.fori_loop(0, CHIPS, chip_step, 0)

    def exchange(src, dst, send, recv, k):
        return pltpu.make_async_remote_copy(
            src_ref=src, dst_ref=dst, send_sem=send, recv_sem=recv,
            device_id=(me_d, peer(k)), device_id_type=MESH,
        )

    mean = means[...]
    square = dot(mean * mean, jnp.where(same, 1.0 / 64.0, 0.0), HI)
    pooled32 = mean / jnp.sqrt(square + EPS)
    pooled = pooled32.astype(BF16)
    projected = dot(pooled, weight).astype(BF16)
    margin_part[...] = dot_t(projected, pooled) - dot_t(pooled, projected)

    def margin_copy(k):
        rows = pl.ds(pl.multiple_of(peer(k) * 8, 8), 8)
        return exchange(margin_part.at[rows], r_margin.at[k], send_b.at[k], recv_b.at[k], k)

    def start_b(k, _):
        margin_copy(k).start()
        return 0

    lax.fori_loop(1, NS, start_b, 0)
    r_margin[0] = margin_part[pl.ds(pl.multiple_of(me * 8, 8), 8), :]
    skew_rows = dot(pooled, skewed).astype(BF16)
    pooled_t = jnp.transpose(pooled.astype(F32)).astype(BF16)
    ranks = jnp.broadcast_to(rank[...].astype(F32), (8, 128))
    mine = iota((8, 128), 1) == me * 8 + iota((8, 128), 0)
    own_rank = jnp.sum(jnp.where(mine, ranks, 0.0), axis=1, keepdims=True)
    target = jnp.where(own_rank < ranks, 1.0, jnp.where(own_rank > ranks, 0.0, 0.5))
    valid = mask[...].astype(F32)

    def wait_b(k, _):
        margin_copy(k).wait()
        return 0

    lax.fori_loop(1, NS, wait_b, 0)
    margin = jnp.sum(r_margin[...], axis=0)
    soft = jnp.maximum(margin, 0.0) + jnp.log(1.0 + jnp.exp(-jnp.abs(margin)))
    losses = jnp.sum(valid * (soft - target * margin), axis=0, keepdims=True)
    pair = 2.0 * valid * (1.0 / (1.0 + jnp.exp(-margin)) - target)
    loss_high = losses.astype(BF16).astype(F32)
    loss_rows = jnp.where(iota((8, 128), 0) == 0, loss_high, losses - loss_high)
    sent = jnp.concatenate([pair, loss_rows], axis=0).astype(BF16)
    pair_own[...] = sent
    r_pair[me] = sent

    def pair_copy(k):
        return exchange(pair_own, r_pair.at[me], send_c.at[k], recv_c.at[k], k)

    def start_c(k, _):
        pair_copy(k).start()
        return 0

    lax.fori_loop(1, NS, start_c, 0)

    def wait_c(k, _):
        pair_copy(k).wait()
        return 0

    lax.fori_loop(1, NS, wait_c, 0)
    pairs = r_pair[...].astype(F32)
    all_pair = pairs[:, :8, :].reshape(128, 128).astype(BF16)
    accumulated = dot(all_pair, pooled)
    high = accumulated.astype(BF16)
    low = (accumulated - high.astype(F32)).astype(BF16)
    product = (dot(pooled_t, high) + dot(pooled_t, low)) * (1.0 / 4096.0)
    for i in range(2 * NS):
        h = i // 8
        piece = product[i * 8 : i * 8 + 8, h * 64 : h * 64 + 64]
        w_part[i] = jnp.concatenate([piece[:4], piece[4:]], axis=1).astype(BF16)

    def w_copy(i):
        to_d = me * 2 + i // NS
        to_s = lax.rem(i, NS)
        return to_d, to_s, pltpu.make_async_remote_copy(
            src_ref=w_part.at[i],
            dst_ref=r_w.at[me_d],
            send_sem=send_w.at[i], recv_sem=recv_w.at[me_d],
            device_id=(to_d, to_s), device_id_type=MESH,
        )

    def start_w(i, _):
        to_d, to_s, c = w_copy(i)
        itself = jnp.logical_and(to_d == me_d, to_s == me)

        @pl.when(jnp.logical_not(itself))
        def _():
            c.start()

        @pl.when(itself)
        def _():
            r_w[me_d] = w_part[i]

        return 0

    lax.fori_loop(0, 2 * NS, start_w, 0)
    grad_part[...] = dot(all_pair, skew_rows).astype(BF16).reshape(NS, 8, 256)

    def grad_copy(k):
        return exchange(grad_part.at[peer(k)], r_grad.at[me], send_d.at[k], recv_d.at[k], k)

    def start_d(k, _):
        grad_copy(k).start()
        return 0

    lax.fori_loop(1, NS, start_d, 0)
    r_grad[me] = grad_part[me]
    loss_o[0] = jnp.sum(pairs[:, 8:10, :]) * (1.0 / (128.0 * 128.0))

    def wait_d(k, _):
        grad_copy(k).wait()
        return 0

    lax.fori_loop(1, NS, wait_d, 0)
    for b in range(NS):
        pg_o[:, b * 256 : b * 256 + 256] = r_grad[b].astype(F32)

    def wait_w(i, _):
        to_d, to_s, c = w_copy(i)

        @pl.when(jnp.logical_not(jnp.logical_and(to_d == me_d, to_s == me)))
        def _():
            c.wait_send()

        arrived = pltpu.make_async_remote_copy(
            src_ref=w_part.at[0], dst_ref=r_w.at[i],
            send_sem=send_w.at[i], recv_sem=recv_w.at[i],
            device_id=(to_d, to_s), device_id_type=MESH,
        )

        @pl.when(jnp.logical_or(i != me_d, home != me))
        def _():
            arrived.wait_recv()

        return 0

    lax.fori_loop(0, ND, wait_w, 0)
    folded = jnp.sum(r_w[...].astype(F32), axis=0)
    wg_o[...] = jnp.concatenate([folded[:, :64], folded[:, 64:]], axis=0)


def per_device(
    token_input, input_map, output_map, step_size, forget, skip_gain, segments, yield_rank,
    pair_mask, comparator,
):
    vmem = pl.BlockSpec(memory_space=pltpu.VMEM)
    smem = pl.BlockSpec(memory_space=pltpu.SMEM)
    shape = jax.ShapeDtypeStruct
    sem = pltpu.SemaphoreType.DMA
    pooled_grad, loss, weight_grad = pl.pallas_call(
        list_kernel,
        out_shape=(shape((8, 4096), F32), shape((1,), F32), shape((8, 64), F32)),
        in_specs=[smem] + [vmem] * 6 + [pl.BlockSpec(memory_space=pl.ANY)] + [vmem] * 2,
        out_specs=(vmem, smem, vmem),
        scratch_shapes=[
            pltpu.VMEM((128, 128), F32),
            pltpu.VMEM((64, 128), F32),
            pltpu.VMEM((8, 160, 256), BF16),
            pltpu.VMEM((8, 16, 256), F32),
            pltpu.VMEM((8, 160, 256), BF16),
            pltpu.VMEM((8, 16, 256), F32),
            pltpu.VMEM((8, 160, 256), BF16),
            pltpu.VMEM((8, 16, 256), F32),
            pltpu.VMEM((7, 192, 256), BF16),
            pltpu.VMEM((8, 192, 256), BF16),
            pltpu.VMEM((64, 256), BF16),
            pltpu.VMEM((128, 256), F32),
            pltpu.VMEM((128, 256), F32),
            pltpu.VMEM((128, 128), F32),
            pltpu.VMEM((16, 8, 128), F32),
            pltpu.VMEM((16, 128), BF16),
            pltpu.VMEM((16, 16, 128), BF16),
            pltpu.VMEM((16, 8, 256), BF16),
            pltpu.VMEM((16, 8, 256), BF16),
            pltpu.VMEM((32, 4, 128), BF16),
            pltpu.VMEM((32, 4, 128), BF16),
            sem((8,)), sem((8,)), sem((8,)), sem((8,)), sem((7,)), sem((7,)),
            sem((16,)), sem((16,)), sem((16,)), sem((16,)), sem((16,)), sem((16,)),
            sem((32,)), sem((32,)), sem(()),
        ],
        compiler_params=pltpu.CompilerParams(collective_id=0, has_side_effects=True),
        name="list",
    )(
        skip_gain, token_input[0], input_map[0], output_map[0], step_size[0].T, forget[0].T,
        segments[0], comparator.T, yield_rank, pair_mask[0],
    )
    return (loss, pooled_grad[None], weight_grad)


def solution(mesh):
    return jax.shard_map(
        per_device,
        mesh=mesh,
        in_specs=(
            P("dp", "seq", None),
            P("dp", "seq", None),
            P("dp", "seq", None),
            P("dp", "seq", None),
            P("dp", "seq", None),
            P(),
            P("dp", "seq", None),
            P("dp", None),
            P("dp", "seq", None),
            P(),
        ),
        out_specs=(P("dp"), P("dp", "seq", None), P(("dp", "seq"), None)),
        check_vma=False,
    )
```

```python
import jax
import jax.numpy as jnp
from jax import lax
from jax.experimental import pallas as pl
from jax.experimental.pallas import tpu as pltpu
from jax.sharding import PartitionSpec as P

HI = lax.Precision.HIGHEST
F32 = jnp.float32
BF16 = jnp.bfloat16
EPS = 1e-05
NS = 16
ND = 32
CHIPS = 8
AHEAD = 2
MESH = pl.DeviceIdType.MESH


def dot(a, b, precision=None):
    return lax.dot_general(
        a, b, (((1,), (0,)), ((), ())), precision=precision, preferred_element_type=F32
    )


def dot_t(a, b):
    return lax.dot_general(a, b, (((1,), (1,)), ((), ())), preferred_element_type=F32)


def iota(shape, axis):
    return lax.broadcasted_iota(jnp.int32, shape, axis)


def list_kernel(
    skip, tok, b_in, c_out, step, forget, seg, w_in, rank, mask,
    pg_o, loss_o, wg_o,
    cols, dl_rows, give_s, give_m, own_s, own_m, got_s, got_m, pack, pack_d,
    r_pack, r_dec, relay, relay_d, w_own,
    carried, means, margin_part, r_margin, pair_own, r_pair, grad_part, r_grad, w_part, r_w,
    send_g, recv_g, send_m, recv_m, send_a, recv_a, send_ad, recv_ad, hop_s, hop_r, send_b, recv_b, send_c, recv_c,
    send_d, recv_d, send_w, recv_w, w_sem,
):
    me_d = lax.axis_index("dp")
    me = lax.axis_index("seq")
    chip = me // 2
    core = lax.rem(me, 2)
    home = me_d // 2

    def peer(k):
        return lax.rem(me + k, NS)

    barrier = pltpu.get_barrier_semaphore()

    def greet_source(s, _):
        @pl.when(jnp.logical_or(s != me_d, home != me))
        def _():
            pl.semaphore_signal(barrier, inc=1, device_id=(s, home), device_id_type=MESH)

        return 0

    lax.fori_loop(0, ND, greet_source, 0)

    def greet(k, _):
        pl.semaphore_signal(barrier, inc=1, device_id=(me_d, peer(k)), device_id_type=MESH)
        return 0

    lax.fori_loop(1, NS, greet, 0)
    w_fetch = pltpu.make_async_copy(
        w_in.at[:, pl.ds(pl.multiple_of(me * 256, 256), 256)], w_own, w_sem
    )
    w_fetch.start()

    upper = iota((128, 128), 0) <= iota((128, 128), 1)
    lower = iota((128, 128), 0) >= iota((128, 128), 1)
    dl = -dot(forget[...], upper.astype(F32), HI)
    end_weight = jnp.exp(dl[:, 127:128] - dl) * step[...]
    dl_rows[...] = dl
    cols[...] = jnp.transpose(jnp.concatenate([dl, end_weight], axis=0))
    b_t = jnp.transpose(b_in[...].astype(F32)).astype(BF16)
    scores = jnp.where(lower, dot_t(c_out[...], b_in[...]), 0.0)
    member = (jnp.broadcast_to(seg[...], (8, 128)) == iota((8, 128), 0)).astype(F32)
    member_low = member.astype(BF16)
    inverse = 1.0 / jnp.sum(member, axis=1, keepdims=True)
    average = member * inverse
    left = iota((128, 128), 1) < 64
    left8 = left[:8]

    def group(j, out_s, out_m, t):
        here = pltpu.roll(cols[...], lax.rem(128 - 4 * j, 128), 1)
        query_rows = []
        for pair in range(2):
            lanes = pl.ds(pl.multiple_of(j * 256 + pair * 128, 128), 128)
            at_lanes = slice(pair * 128, pair * 128 + 128)
            tokens = tok[:, lanes]
            mixed = []
            totals = []
            for i in range(2):
                at = pair * 2 + i
                row = dl_rows[pl.ds(j * 4 + at, 1), :]
                gap = here[:, at : at + 1] - row
                mixing = scores * jnp.exp(jnp.minimum(gap, 0.0)) * step[pl.ds(j * 4 + at, 1), :]
                mixed.append(dot(member_low, mixing.astype(BF16)) + skip[j * 4 + at] * member)
                past = jnp.exp(row)
                query_rows.append(average * past)
                totals.append(past[:, 127:128])
            both = dot(jnp.concatenate(mixed, axis=0).astype(BF16), tokens)
            out_m[t, 0:8, at_lanes] = jnp.where(left8, both[:8], both[8:]) * inverse
            out_m[t, 8:16, at_lanes] = jnp.where(left8, totals[0], totals[1])
            base = 64 + pair * 2
            weight = jnp.where(left, here[:, base : base + 1], here[:, base + 1 : base + 2])
            scaled = (tokens.astype(F32) * weight).astype(BF16)
            out_s[t, 0:128, at_lanes] = dot(b_t, scaled).astype(BF16)
        queries = dot(jnp.concatenate(query_rows, axis=0).astype(BF16), c_out[...]).astype(BF16)
        out_s[t, 128:160, 0:128] = queries
        out_s[t, 128:160, 128:256] = queries

    def target_chip(t):
        away = CHIPS // 2 + (t // 2 + lax.rem(t, 2)) * (1 - 2 * lax.rem(t, 2))
        return lax.rem(chip + away, CHIPS)

    def compute(t, _):
        to = target_chip(t) * 2
        group(to + 1 - core, give_s, give_m, t)
        group(to + core, own_s, own_m, t)
        return 0

    def give(t):
        other = (me_d, chip * 2 + 1 - core)
        return (
            pltpu.make_async_remote_copy(
                src_ref=give_s.at[t], dst_ref=got_s.at[t], send_sem=send_g.at[t],
                recv_sem=recv_g.at[t], device_id=other, device_id_type=MESH,
            ),
            pltpu.make_async_remote_copy(
                src_ref=give_m.at[t], dst_ref=got_m.at[t], send_sem=send_m.at[t],
                recv_sem=recv_m.at[t], device_id=other, device_id_type=MESH,
            ),
        )

    def send_give(t, _):
        for c in give(t):
            c.start()
        return 0

    lane = iota((8, 256), 1) // 64

    def by_head(rows):
        total = jnp.where(lane == 0, rows[0:8], 0.0)
        for h in range(1, 4):
            total = total + jnp.where(lane == h, rows[h * 8 : h * 8 + 8], 0.0)
        return total

    def combine(t, out, out_d, at):
        for c in give(t):
            c.wait()
        first = core == 0
        mine, theirs = own_s[t], got_s[t]
        early = jnp.where(first, mine, theirs)
        late = jnp.where(first, theirs, mine)
        mine_m, theirs_m = own_m[t], got_m[t]
        early_m = jnp.where(first, mine_m, theirs_m)
        late_m = jnp.where(first, theirs_m, mine_m)
        early_d, late_d = early_m[8:9, :], late_m[8:9, :]
        state = late_d * early[:128].astype(F32) + late[:128].astype(F32)
        late_q = late[128:160, 0:128]
        within = by_head(dot(late_q, early[:128]))
        scaled_q = late_q.astype(F32)
        scaled_q = jnp.concatenate(
            [scaled_q[h * 8 : h * 8 + 8] * early_d[:, h * 64 : h * 64 + 1] for h in range(4)],
            axis=0,
        )
        out[at, 0:128, :] = state.astype(BF16)
        out[at, 128:160, 0:128] = early[128:160, 0:128]
        out[at, 128:160, 128:256] = scaled_q.astype(BF16)
        out[at, 160:176, :] = jnp.concatenate(
            [early_m[0:8], late_m[0:8] + within], axis=0
        ).astype(BF16)
        decay = early_d * late_d
        out_d[at] = jnp.concatenate([decay[:, :128], decay[:, 128:]], axis=0)

    def package(t):
        to = (me_d, target_chip(t) * 2 + core)
        return (
            pltpu.make_async_remote_copy(
                src_ref=pack.at[t], dst_ref=r_pack.at[chip], send_sem=send_a.at[t],
                recv_sem=recv_a.at[t], device_id=to, device_id_type=MESH,
            ),
            pltpu.make_async_remote_copy(
                src_ref=pack_d.at[t], dst_ref=r_dec.at[chip], send_sem=send_ad.at[t],
                recv_sem=recv_ad.at[t], device_id=to, device_id_type=MESH,
            ),
        )

    way = 1 - 2 * core

    def chip_at(away):
        return lax.rem(chip + away * way + CHIPS, CHIPS)

    hop_to = (me_d, chip_at(1) * 2 + core)
    to_relay = (
        pltpu.make_async_remote_copy(
            src_ref=pack.at[0], dst_ref=relay, send_sem=hop_s.at[0], recv_sem=hop_r.at[0],
            device_id=hop_to, device_id_type=MESH,
        ),
        pltpu.make_async_remote_copy(
            src_ref=pack_d.at[0], dst_ref=relay_d, send_sem=hop_s.at[1], recv_sem=hop_r.at[1],
            device_id=hop_to, device_id_type=MESH,
        ),
    )
    end_at = (me_d, chip_at(3) * 2 + core)
    origin = chip_at(-1)
    forward = (
        pltpu.make_async_remote_copy(
            src_ref=relay, dst_ref=r_pack.at[origin], send_sem=send_a.at[0],
            recv_sem=recv_a.at[0], device_id=end_at, device_id_type=MESH,
        ),
        pltpu.make_async_remote_copy(
            src_ref=relay_d, dst_ref=r_dec.at[origin], send_sem=send_ad.at[0],
            recv_sem=recv_ad.at[0], device_id=end_at, device_id_type=MESH,
        ),
    )

    def send_package(t):
        @pl.when(t == 0)
        def _():
            for c in to_relay:
                c.start()

        @pl.when(t > 0)
        def _():
            for c in package(t):
                c.start()

    lax.fori_loop(0, AHEAD, compute, 0)
    pl.semaphore_wait(barrier, NS - 1 + ND - (home == me).astype(jnp.int32))
    lax.fori_loop(0, AHEAD, send_give, 0)

    def middle(t, _):
        combine(t - AHEAD, pack, pack_d, t - AHEAD)
        compute(t, 0)
        send_package(t - AHEAD)
        send_give(t, 0)
        return 0

    lax.fori_loop(AHEAD, CHIPS, middle, 0)
    combine(CHIPS - AHEAD, pack, pack_d, CHIPS - AHEAD)
    for c in to_relay:
        c.wait_recv()
    for c in forward:
        c.start()

    def rest(t, _):
        combine(t, pack, pack_d, t)
        send_package(t - 1)
        return 0

    lax.fori_loop(CHIPS - AHEAD + 1, CHIPS - 1, rest, 0)
    combine(CHIPS - 1, r_pack, r_dec, chip)
    for c in package(CHIPS - 2):
        c.start()

    w_fetch.wait()
    narrow = w_own[...].astype(F32)
    same = (iota((256, 256), 0) // 64) == (iota((256, 256), 1) // 64)
    blocks_t = jnp.where(same, jnp.concatenate([narrow, narrow, narrow, narrow], axis=0), 0.0)
    blocks = jnp.transpose(blocks_t)
    weight = blocks.astype(BF16)
    skewed = (blocks_t - blocks).astype(BF16)
    carried[...] = jnp.zeros_like(carried)

    def chip_step(b, _):
        away = lax.rem(chip - b + CHIPS, CHIPS)
        half = CHIPS // 2
        order = jnp.where(away < half, CHIPS - 1 - 2 * away, 2 * (away - half))

        @pl.when(b != chip)
        def _():
            for c in package(order):
                c.wait_recv()

        now = carried[...]
        queries = jnp.concatenate([r_pack[b, 128:160, 0:128], r_pack[b, 128:160, 128:256]], axis=0)
        past = dot(queries, now.astype(BF16))
        local = r_pack[b, 160:176, :].astype(F32)
        means[pl.ds(pl.multiple_of(b * 16, 16), 16), :] = local + jnp.concatenate(
            [by_head(past[:32]), by_head(past[32:])], axis=0
        )
        decay = jnp.concatenate([r_dec[b, 0:1, :], r_dec[b, 1:2, :]], axis=1)
        carried[...] = decay * now + r_pack[b, 0:128, :].astype(F32)
        return 0

    lax.fori_loop(0, CHIPS, chip_step, 0)

    def exchange(src, dst, send, recv, k):
        return pltpu.make_async_remote_copy(
            src_ref=src, dst_ref=dst, send_sem=send, recv_sem=recv,
            device_id=(me_d, peer(k)), device_id_type=MESH,
        )

    mean = means[...]
    square = dot(mean * mean, jnp.where(same, 1.0 / 64.0, 0.0), HI)
    pooled32 = mean / jnp.sqrt(square + EPS)
    pooled = pooled32.astype(BF16)
    projected = dot(pooled, weight).astype(BF16)
    margin_part[...] = dot_t(projected, pooled) - dot_t(pooled, projected)

    def margin_copy(k):
        rows = pl.ds(pl.multiple_of(peer(k) * 8, 8), 8)
        return exchange(margin_part.at[rows], r_margin.at[k], send_b.at[k], recv_b.at[k], k)

    def start_b(k, _):
        margin_copy(k).start()
        return 0

    lax.fori_loop(1, NS, start_b, 0)
    r_margin[0] = margin_part[pl.ds(pl.multiple_of(me * 8, 8), 8), :]
    skew_rows = dot(pooled, skewed).astype(BF16)
    pooled_t = jnp.transpose(pooled.astype(F32)).astype(BF16)
    ranks = jnp.broadcast_to(rank[...].astype(F32), (8, 128))
    mine = iota((8, 128), 1) == me * 8 + iota((8, 128), 0)
    own_rank = jnp.sum(jnp.where(mine, ranks, 0.0), axis=1, keepdims=True)
    target = jnp.where(own_rank < ranks, 1.0, jnp.where(own_rank > ranks, 0.0, 0.5))
    valid = mask[...].astype(F32)

    def wait_b(k, _):
        margin_copy(k).wait()
        return 0

    lax.fori_loop(1, NS, wait_b, 0)
    margin = jnp.sum(r_margin[...], axis=0)
    soft = jnp.maximum(margin, 0.0) + jnp.log(1.0 + jnp.exp(-jnp.abs(margin)))
    losses = jnp.sum(valid * (soft - target * margin), axis=0, keepdims=True)
    pair = 2.0 * valid * (1.0 / (1.0 + jnp.exp(-margin)) - target)
    loss_high = losses.astype(BF16).astype(F32)
    loss_rows = jnp.where(iota((8, 128), 0) == 0, loss_high, losses - loss_high)
    sent = jnp.concatenate([pair, loss_rows], axis=0).astype(BF16)
    pair_own[...] = sent
    r_pair[me] = sent

    def pair_copy(k):
        return exchange(pair_own, r_pair.at[me], send_c.at[k], recv_c.at[k], k)

    def start_c(k, _):
        pair_copy(k).start()
        return 0

    lax.fori_loop(1, NS, start_c, 0)

    def wait_c(k, _):
        pair_copy(k).wait()
        return 0

    lax.fori_loop(1, NS, wait_c, 0)
    pairs = r_pair[...].astype(F32)
    all_pair = pairs[:, :8, :].reshape(128, 128).astype(BF16)
    accumulated = dot(all_pair, pooled)
    high = accumulated.astype(BF16)
    low = (accumulated - high.astype(F32)).astype(BF16)
    product = (dot(pooled_t, high) + dot(pooled_t, low)) * (1.0 / 4096.0)
    for i in range(2 * NS):
        h = i // 8
        piece = product[i * 8 : i * 8 + 8, h * 64 : h * 64 + 64]
        w_part[i] = jnp.concatenate([piece[:4], piece[4:]], axis=1).astype(BF16)

    def w_copy(i):
        to_d = me * 2 + i // NS
        to_s = lax.rem(i, NS)
        return to_d, to_s, pltpu.make_async_remote_copy(
            src_ref=w_part.at[i],
            dst_ref=r_w.at[me_d],
            send_sem=send_w.at[i], recv_sem=recv_w.at[me_d],
            device_id=(to_d, to_s), device_id_type=MESH,
        )

    def start_w(i, _):
        to_d, to_s, c = w_copy(i)
        itself = jnp.logical_and(to_d == me_d, to_s == me)

        @pl.when(jnp.logical_not(itself))
        def _():
            c.start()

        @pl.when(itself)
        def _():
            r_w[me_d] = w_part[i]

        return 0

    lax.fori_loop(0, 2 * NS, start_w, 0)
    grad_part[...] = dot(all_pair, skew_rows).astype(BF16).reshape(NS, 8, 256)

    def grad_copy(k):
        return exchange(grad_part.at[peer(k)], r_grad.at[me], send_d.at[k], recv_d.at[k], k)

    def start_d(k, _):
        grad_copy(k).start()
        return 0

    lax.fori_loop(1, NS, start_d, 0)
    r_grad[me] = grad_part[me]
    loss_o[0] = jnp.sum(pairs[:, 8:10, :]) * (1.0 / (128.0 * 128.0))

    for c in to_relay:
        c.wait_send()

    def wait_a(t, _):
        for c in package(t):
            c.wait_send()
        return 0

    lax.fori_loop(0, CHIPS - 1, wait_a, 0)

    def wait_d(k, _):
        grad_copy(k).wait()
        return 0

    lax.fori_loop(1, NS, wait_d, 0)
    for b in range(NS):
        pg_o[:, b * 256 : b * 256 + 256] = r_grad[b]

    def wait_w(i, _):
        to_d, to_s, c = w_copy(i)

        @pl.when(jnp.logical_not(jnp.logical_and(to_d == me_d, to_s == me)))
        def _():
            c.wait_send()

        arrived = pltpu.make_async_remote_copy(
            src_ref=w_part.at[0], dst_ref=r_w.at[i],
            send_sem=send_w.at[i], recv_sem=recv_w.at[i],
            device_id=(to_d, to_s), device_id_type=MESH,
        )

        @pl.when(jnp.logical_or(i != me_d, home != me))
        def _():
            arrived.wait_recv()

        return 0

    lax.fori_loop(0, ND, wait_w, 0)
    folded = jnp.sum(r_w[...].astype(F32), axis=0)
    wg_o[...] = jnp.concatenate([folded[:, :64], folded[:, 64:]], axis=0)


def per_device(
    token_input, input_map, output_map, step_size, forget, skip_gain, segments, yield_rank,
    pair_mask, comparator,
):
    vmem = pl.BlockSpec(memory_space=pltpu.VMEM)
    smem = pl.BlockSpec(memory_space=pltpu.SMEM)
    shape = jax.ShapeDtypeStruct
    sem = pltpu.SemaphoreType.DMA
    pooled_grad, loss, weight_grad = pl.pallas_call(
        list_kernel,
        out_shape=(shape((8, 4096), BF16), shape((1,), F32), shape((8, 64), F32)),
        in_specs=[smem] + [vmem] * 6 + [pl.BlockSpec(memory_space=pl.ANY)] + [vmem] * 2,
        out_specs=(vmem, smem, vmem),
        scratch_shapes=[
            pltpu.VMEM((128, 128), F32),
            pltpu.VMEM((64, 128), F32),
            pltpu.VMEM((8, 160, 256), BF16),
            pltpu.VMEM((8, 16, 256), F32),
            pltpu.VMEM((8, 160, 256), BF16),
            pltpu.VMEM((8, 16, 256), F32),
            pltpu.VMEM((8, 160, 256), BF16),
            pltpu.VMEM((8, 16, 256), F32),
            pltpu.VMEM((7, 176, 256), BF16),
            pltpu.VMEM((7, 2, 128), F32),
            pltpu.VMEM((8, 176, 256), BF16),
            pltpu.VMEM((8, 2, 128), F32),
            pltpu.VMEM((176, 256), BF16),
            pltpu.VMEM((2, 128), F32),
            pltpu.VMEM((64, 256), BF16),
            pltpu.VMEM((128, 256), F32),
            pltpu.VMEM((128, 256), F32),
            pltpu.VMEM((128, 128), F32),
            pltpu.VMEM((16, 8, 128), F32),
            pltpu.VMEM((16, 128), BF16),
            pltpu.VMEM((16, 16, 128), BF16),
            pltpu.VMEM((16, 8, 256), BF16),
            pltpu.VMEM((16, 8, 256), BF16),
            pltpu.VMEM((32, 4, 128), BF16),
            pltpu.VMEM((32, 4, 128), BF16),
            sem((8,)), sem((8,)), sem((8,)), sem((8,)), sem((7,)), sem((7,)),
            sem((7,)), sem((7,)), sem((2,)), sem((2,)),
            sem((16,)), sem((16,)), sem((16,)), sem((16,)), sem((16,)), sem((16,)),
            sem((32,)), sem((32,)), sem(()),
        ],
        compiler_params=pltpu.CompilerParams(collective_id=0, has_side_effects=True),
        name="list",
    )(
        skip_gain, token_input[0], input_map[0], output_map[0], step_size[0].T, forget[0].T,
        segments[0], comparator.T, yield_rank, pair_mask[0],
    )
    return (loss, pooled_grad.astype(F32)[None], weight_grad)


def solution(mesh):
    return jax.shard_map(
        per_device,
        mesh=mesh,
        in_specs=(
            P("dp", "seq", None),
            P("dp", "seq", None),
            P("dp", "seq", None),
            P("dp", "seq", None),
            P("dp", "seq", None),
            P(),
            P("dp", "seq", None),
            P("dp", None),
            P("dp", "seq", None),
            P(),
        ),
        out_specs=(P("dp"), P("dp", "seq", None), P(("dp", "seq"), None)),
        check_vma=False,
    )
```

```python
import jax
import jax.numpy as jnp
from jax import lax
from jax.experimental import pallas as pl
from jax.experimental.pallas import tpu as pltpu
from jax.sharding import PartitionSpec as P

HI = lax.Precision.HIGHEST
F32 = jnp.float32
BF16 = jnp.bfloat16
EPS = 1e-05
NS = 16
ND = 32
COLS = 4
CHIPS = 8
AHEAD = 2
MESH = pl.DeviceIdType.MESH


def dot(a, b, precision=None):
    return lax.dot_general(
        a, b, (((1,), (0,)), ((), ())), precision=precision, preferred_element_type=F32
    )


def dot_t(a, b):
    return lax.dot_general(a, b, (((1,), (1,)), ((), ())), preferred_element_type=F32)


def iota(shape, axis):
    return lax.broadcasted_iota(jnp.int32, shape, axis)


def list_kernel(
    skip, tok, b_in, c_out, step, forget, seg, w_in, rank, mask,
    pg_o, loss_o, wg_o,
    cols, dl_rows, give_s, give_m, own_s, own_m, got_s, got_m, pack, pack_d,
    r_pack, r_dec, relay, relay_d, w_own,
    carried, means, margin_part, r_margin, pair_own, r_pair, grad_part, r_grad, w_part, r_w,
    send_g, recv_g, send_m, recv_m, send_a, recv_a, send_ad, recv_ad, hop_s, hop_r, send_b, recv_b, send_c, recv_c,
    send_d, recv_d, send_w, recv_w, w_sem, line_sem, plane_sem,
):
    me_d = lax.axis_index("dp")
    me = lax.axis_index("seq")
    chip = me // 2
    core = lax.rem(me, 2)
    home = me_d // 2

    def peer(k):
        return lax.rem(me + k, NS)

    barrier = pltpu.get_barrier_semaphore()

    def greet(k, _):
        pl.semaphore_signal(barrier, inc=1, device_id=(me_d, peer(k)), device_id_type=MESH)
        return 0

    lax.fori_loop(1, NS, greet, 0)
    rows_y, cols_x = ND // COLS, COLS
    at_y, at_x = me_d // COLS, lax.rem(me_d, COLS)
    for k in range(1, rows_y):
        there = lax.rem(at_y + k, rows_y) * COLS + at_x
        pl.semaphore_signal(barrier, inc=1, device_id=(there, me), device_id_type=MESH)
    beside = [(at_y * COLS + lax.rem(at_x + k, cols_x), me) for k in range(1, cols_x)]
    for there in beside:
        pl.semaphore_signal(barrier, inc=1, device_id=there, device_id_type=MESH)
    w_fetch = pltpu.make_async_copy(
        w_in.at[:, pl.ds(pl.multiple_of(me * 256, 256), 256)], w_own, w_sem
    )
    w_fetch.start()

    upper = iota((128, 128), 0) <= iota((128, 128), 1)
    lower = iota((128, 128), 0) >= iota((128, 128), 1)
    dl = -dot(forget[...], upper.astype(F32), HI)
    end_weight = jnp.exp(dl[:, 127:128] - dl) * step[...]
    dl_rows[...] = dl
    cols[...] = jnp.transpose(jnp.concatenate([dl, end_weight], axis=0))
    b_t = jnp.transpose(b_in[...].astype(F32)).astype(BF16)
    scores = jnp.where(lower, dot_t(c_out[...], b_in[...]), 0.0)
    member = (jnp.broadcast_to(seg[...], (8, 128)) == iota((8, 128), 0)).astype(F32)
    member_low = member.astype(BF16)
    inverse = 1.0 / jnp.sum(member, axis=1, keepdims=True)
    average = member * inverse
    left = iota((128, 128), 1) < 64
    left8 = left[:8]

    def group(j, out_s, out_m, t):
        here = pltpu.roll(cols[...], lax.rem(128 - 4 * j, 128), 1)
        query_rows = []
        for pair in range(2):
            lanes = pl.ds(pl.multiple_of(j * 256 + pair * 128, 128), 128)
            at_lanes = slice(pair * 128, pair * 128 + 128)
            tokens = tok[:, lanes]
            mixed = []
            totals = []
            for i in range(2):
                at = pair * 2 + i
                row = dl_rows[pl.ds(j * 4 + at, 1), :]
                gap = here[:, at : at + 1] - row
                mixing = scores * jnp.exp(jnp.minimum(gap, 0.0)) * step[pl.ds(j * 4 + at, 1), :]
                mixed.append(dot(member_low, mixing.astype(BF16)) + skip[j * 4 + at] * member)
                past = jnp.exp(row)
                query_rows.append(average * past)
                totals.append(past[:, 127:128])
            both = dot(jnp.concatenate(mixed, axis=0).astype(BF16), tokens)
            out_m[t, 0:8, at_lanes] = jnp.where(left8, both[:8], both[8:]) * inverse
            out_m[t, 8:16, at_lanes] = jnp.where(left8, totals[0], totals[1])
            base = 64 + pair * 2
            weight = jnp.where(left, here[:, base : base + 1], here[:, base + 1 : base + 2])
            scaled = (tokens.astype(F32) * weight).astype(BF16)
            out_s[t, 0:128, at_lanes] = dot(b_t, scaled).astype(BF16)
        queries = dot(jnp.concatenate(query_rows, axis=0).astype(BF16), c_out[...]).astype(BF16)
        out_s[t, 128:160, 0:128] = queries
        out_s[t, 128:160, 128:256] = queries

    def target_chip(t):
        away = CHIPS // 2 + (t // 2 + lax.rem(t, 2)) * (1 - 2 * lax.rem(t, 2))
        return lax.rem(chip + away, CHIPS)

    def compute(t, _):
        to = target_chip(t) * 2
        group(to + 1 - core, give_s, give_m, t)
        group(to + core, own_s, own_m, t)
        return 0

    def give(t):
        other = (me_d, chip * 2 + 1 - core)
        return (
            pltpu.make_async_remote_copy(
                src_ref=give_s.at[t], dst_ref=got_s.at[t], send_sem=send_g.at[t],
                recv_sem=recv_g.at[t], device_id=other, device_id_type=MESH,
            ),
            pltpu.make_async_remote_copy(
                src_ref=give_m.at[t], dst_ref=got_m.at[t], send_sem=send_m.at[t],
                recv_sem=recv_m.at[t], device_id=other, device_id_type=MESH,
            ),
        )

    def send_give(t, _):
        for c in give(t):
            c.start()
        return 0

    lane = iota((8, 256), 1) // 64

    def by_head(rows):
        total = jnp.where(lane == 0, rows[0:8], 0.0)
        for h in range(1, 4):
            total = total + jnp.where(lane == h, rows[h * 8 : h * 8 + 8], 0.0)
        return total

    def combine(t, out, out_d, at):
        for c in give(t):
            c.wait()
        first = core == 0
        mine, theirs = own_s[t], got_s[t]
        early = jnp.where(first, mine, theirs)
        late = jnp.where(first, theirs, mine)
        mine_m, theirs_m = own_m[t], got_m[t]
        early_m = jnp.where(first, mine_m, theirs_m)
        late_m = jnp.where(first, theirs_m, mine_m)
        early_d, late_d = early_m[8:9, :], late_m[8:9, :]
        state = late_d * early[:128].astype(F32) + late[:128].astype(F32)
        late_q = late[128:160, 0:128]
        within = by_head(dot(late_q, early[:128]))
        scaled_q = late_q.astype(F32)
        scaled_q = jnp.concatenate(
            [scaled_q[h * 8 : h * 8 + 8] * early_d[:, h * 64 : h * 64 + 1] for h in range(4)],
            axis=0,
        )
        out[at, 0:128, :] = state.astype(BF16)
        out[at, 128:160, 0:128] = early[128:160, 0:128]
        out[at, 128:160, 128:256] = scaled_q.astype(BF16)
        out[at, 160:176, :] = jnp.concatenate(
            [early_m[0:8], late_m[0:8] + within], axis=0
        ).astype(BF16)
        decay = early_d * late_d
        out_d[at] = jnp.concatenate([decay[:, :128], decay[:, 128:]], axis=0)

    def package(t):
        to = (me_d, target_chip(t) * 2 + core)
        return (
            pltpu.make_async_remote_copy(
                src_ref=pack.at[t], dst_ref=r_pack.at[chip], send_sem=send_a.at[t],
                recv_sem=recv_a.at[t], device_id=to, device_id_type=MESH,
            ),
            pltpu.make_async_remote_copy(
                src_ref=pack_d.at[t], dst_ref=r_dec.at[chip], send_sem=send_ad.at[t],
                recv_sem=recv_ad.at[t], device_id=to, device_id_type=MESH,
            ),
        )

    way = 1 - 2 * core

    def chip_at(away):
        return lax.rem(chip + away * way + CHIPS, CHIPS)

    hop_to = (me_d, chip_at(1) * 2 + core)
    to_relay = (
        pltpu.make_async_remote_copy(
            src_ref=pack.at[0], dst_ref=relay, send_sem=hop_s.at[0], recv_sem=hop_r.at[0],
            device_id=hop_to, device_id_type=MESH,
        ),
        pltpu.make_async_remote_copy(
            src_ref=pack_d.at[0], dst_ref=relay_d, send_sem=hop_s.at[1], recv_sem=hop_r.at[1],
            device_id=hop_to, device_id_type=MESH,
        ),
    )
    end_at = (me_d, chip_at(3) * 2 + core)
    origin = chip_at(-1)
    forward = (
        pltpu.make_async_remote_copy(
            src_ref=relay, dst_ref=r_pack.at[origin], send_sem=send_a.at[0],
            recv_sem=recv_a.at[0], device_id=end_at, device_id_type=MESH,
        ),
        pltpu.make_async_remote_copy(
            src_ref=relay_d, dst_ref=r_dec.at[origin], send_sem=send_ad.at[0],
            recv_sem=recv_ad.at[0], device_id=end_at, device_id_type=MESH,
        ),
    )

    def send_package(t):
        @pl.when(t == 0)
        def _():
            for c in to_relay:
                c.start()

        @pl.when(t > 0)
        def _():
            for c in package(t):
                c.start()

    lax.fori_loop(0, AHEAD, compute, 0)
    pl.semaphore_wait(barrier, NS - 1 + rows_y - 1 + cols_x - 1)
    for there in beside:
        pl.semaphore_signal(line_sem, inc=1, device_id=there, device_id_type=MESH)
    lax.fori_loop(0, AHEAD, send_give, 0)

    def middle(t, _):
        combine(t - AHEAD, pack, pack_d, t - AHEAD)
        compute(t, 0)
        send_package(t - AHEAD)
        send_give(t, 0)
        return 0

    lax.fori_loop(AHEAD, CHIPS, middle, 0)
    combine(CHIPS - AHEAD, pack, pack_d, CHIPS - AHEAD)
    for c in to_relay:
        c.wait_recv()
    for c in forward:
        c.start()

    def rest(t, _):
        combine(t, pack, pack_d, t)
        send_package(t - 1)
        return 0

    lax.fori_loop(CHIPS - AHEAD + 1, CHIPS - 1, rest, 0)
    combine(CHIPS - 1, r_pack, r_dec, chip)
    for c in package(CHIPS - 2):
        c.start()

    pl.semaphore_wait(line_sem, cols_x - 1)

    def tell(k, _):
        pl.semaphore_signal(plane_sem, inc=1, device_id=(me_d, peer(k)), device_id_type=MESH)
        return 0

    lax.fori_loop(1, NS, tell, 0)
    w_fetch.wait()
    narrow = w_own[...].astype(F32)
    same = (iota((256, 256), 0) // 64) == (iota((256, 256), 1) // 64)
    blocks_t = jnp.where(same, jnp.concatenate([narrow, narrow, narrow, narrow], axis=0), 0.0)
    blocks = jnp.transpose(blocks_t)
    weight = blocks.astype(BF16)
    skewed = (blocks_t - blocks).astype(BF16)
    spread = jnp.where(same, 1.0 / 64.0, 0.0).astype(BF16)
    carried[...] = jnp.zeros_like(carried)

    def chip_step(b, _):
        away = lax.rem(chip - b + CHIPS, CHIPS)
        half = CHIPS // 2
        order = jnp.where(away < half, CHIPS - 1 - 2 * away, 2 * (away - half))

        @pl.when(b != chip)
        def _():
            for c in package(order):
                c.wait_recv()

        now = carried[...]
        queries = jnp.concatenate([r_pack[b, 128:160, 0:128], r_pack[b, 128:160, 128:256]], axis=0)
        past = dot(queries, now.astype(BF16))
        local = r_pack[b, 160:176, :].astype(F32)
        means[pl.ds(pl.multiple_of(b * 16, 16), 16), :] = local + jnp.concatenate(
            [by_head(past[:32]), by_head(past[32:])], axis=0
        )
        decay = jnp.concatenate([r_dec[b, 0:1, :], r_dec[b, 1:2, :]], axis=1)
        carried[...] = decay * now + r_pack[b, 0:128, :].astype(F32)
        return 0

    lax.fori_loop(0, CHIPS, chip_step, 0)

    def exchange(src, dst, send, recv, k):
        return pltpu.make_async_remote_copy(
            src_ref=src, dst_ref=dst, send_sem=send, recv_sem=recv,
            device_id=(me_d, peer(k)), device_id_type=MESH,
        )

    mean = means[...]
    squared = mean * mean
    squared_high = squared.astype(BF16)
    squared_low = (squared - squared_high.astype(F32)).astype(BF16)
    square = dot(squared_high, spread) + dot(squared_low, spread)
    pooled = (mean * lax.rsqrt(square + EPS)).astype(BF16)
    projected = dot(pooled, weight).astype(BF16)
    margin_part[...] = dot_t(projected, pooled) - dot_t(pooled, projected)

    def margin_copy(k):
        rows = pl.ds(pl.multiple_of(peer(k) * 8, 8), 8)
        return exchange(margin_part.at[rows], r_margin.at[k], send_b.at[k], recv_b.at[k], k)

    def start_b(k, _):
        margin_copy(k).start()
        return 0

    lax.fori_loop(1, NS, start_b, 0, unroll=True)
    r_margin[0] = margin_part[pl.ds(pl.multiple_of(me * 8, 8), 8), :]
    skew_rows = dot(pooled, skewed).astype(BF16)
    pooled_t = jnp.transpose(pooled.astype(F32)).astype(BF16)
    ranks = jnp.broadcast_to(rank[...].astype(F32), (8, 128))
    mine = iota((8, 128), 1) == me * 8 + iota((8, 128), 0)
    own_rank = jnp.sum(jnp.where(mine, ranks, 0.0), axis=1, keepdims=True)
    target = jnp.where(own_rank < ranks, 1.0, jnp.where(own_rank > ranks, 0.0, 0.5))
    valid = mask[...].astype(F32)

    def wait_b(k, _):
        margin_copy(k).wait()
        return 0

    lax.fori_loop(1, NS, wait_b, 0)
    margin = jnp.sum(r_margin[...], axis=0)
    soft = jnp.maximum(margin, 0.0) + jnp.log(1.0 + jnp.exp(-jnp.abs(margin)))
    losses = jnp.sum(valid * (soft - target * margin), axis=0, keepdims=True)
    pair = 2.0 * valid * (1.0 / (1.0 + jnp.exp(-margin)) - target)
    loss_high = losses.astype(BF16).astype(F32)
    loss_rows = jnp.where(iota((8, 128), 0) == 0, loss_high, losses - loss_high)
    sent = jnp.concatenate([pair, loss_rows], axis=0).astype(BF16)
    pair_own[...] = sent
    r_pair[me] = sent

    def pair_copy(k):
        return exchange(pair_own, r_pair.at[me], send_c.at[k], recv_c.at[k], k)

    def start_c(k, _):
        pair_copy(k).start()
        return 0

    lax.fori_loop(1, NS, start_c, 0, unroll=True)

    pl.semaphore_wait(plane_sem, NS - 1)

    def wait_c(k, _):
        pair_copy(k).wait()
        return 0

    lax.fori_loop(1, NS, wait_c, 0)
    pairs = r_pair[...].astype(F32)
    all_pair = pairs[:, :8, :].reshape(128, 128).astype(BF16)
    accumulated = dot(all_pair, pooled)
    high = accumulated.astype(BF16)
    low = (accumulated - high.astype(F32)).astype(BF16)
    product = (dot(pooled_t, high) + dot(pooled_t, low)) * (1.0 / 4096.0)
    for i in range(2 * NS):
        h = i // 8
        piece = product[i * 8 : i * 8 + 8, h * 64 : h * 64 + 64]
        w_part[i] = jnp.concatenate([piece[:4], piece[4:]], axis=1).astype(BF16)

    def w_copy(i):
        to_d = me * 2 + i // NS
        to_s = lax.rem(i, NS)
        return to_d, to_s, pltpu.make_async_remote_copy(
            src_ref=w_part.at[i],
            dst_ref=r_w.at[me_d],
            send_sem=send_w.at[i], recv_sem=recv_w.at[me_d],
            device_id=(to_d, to_s), device_id_type=MESH,
        )

    def start_w(i, _):
        to_d, to_s, c = w_copy(i)
        itself = jnp.logical_and(to_d == me_d, to_s == me)

        @pl.when(jnp.logical_not(itself))
        def _():
            c.start()

        @pl.when(itself)
        def _():
            r_w[me_d] = w_part[i]

        return 0

    lax.fori_loop(0, 2 * NS, start_w, 0, unroll=4)
    grad_part[...] = dot(all_pair, skew_rows).astype(BF16).reshape(NS, 8, 256)

    def grad_copy(k):
        return exchange(grad_part.at[peer(k)], r_grad.at[me], send_d.at[k], recv_d.at[k], k)

    def start_d(k, _):
        grad_copy(k).start()
        return 0

    lax.fori_loop(1, NS, start_d, 0, unroll=True)
    r_grad[me] = grad_part[me]
    loss_o[0] = jnp.sum(pairs[:, 8:10, :]) * (1.0 / (128.0 * 128.0))

    for c in to_relay:
        c.wait_send()

    def wait_a(t, _):
        for c in package(t):
            c.wait_send()
        return 0

    lax.fori_loop(0, CHIPS - 1, wait_a, 0)

    def wait_d(k, _):
        grad_copy(k).wait()
        return 0

    lax.fori_loop(1, NS, wait_d, 0)
    for b in range(NS):
        pg_o[:, b * 256 : b * 256 + 256] = r_grad[b]

    def wait_w(i, _):
        to_d, to_s, c = w_copy(i)

        @pl.when(jnp.logical_not(jnp.logical_and(to_d == me_d, to_s == me)))
        def _():
            c.wait_send()

        arrived = pltpu.make_async_remote_copy(
            src_ref=w_part.at[0], dst_ref=r_w.at[i],
            send_sem=send_w.at[i], recv_sem=recv_w.at[i],
            device_id=(to_d, to_s), device_id_type=MESH,
        )

        @pl.when(jnp.logical_or(i != me_d, home != me))
        def _():
            arrived.wait_recv()

        return 0

    lax.fori_loop(0, ND, wait_w, 0)
    folded = jnp.sum(r_w[...].astype(F32), axis=0)
    wg_o[...] = jnp.concatenate([folded[:, :64], folded[:, 64:]], axis=0)


def per_device(
    token_input, input_map, output_map, step_size, forget, skip_gain, segments, yield_rank,
    pair_mask, comparator,
):
    vmem = pl.BlockSpec(memory_space=pltpu.VMEM)
    smem = pl.BlockSpec(memory_space=pltpu.SMEM)
    shape = jax.ShapeDtypeStruct
    sem = pltpu.SemaphoreType.DMA
    pooled_grad, loss, weight_grad = pl.pallas_call(
        list_kernel,
        out_shape=(shape((8, 4096), BF16), shape((1,), F32), shape((8, 64), F32)),
        in_specs=[smem] + [vmem] * 6 + [pl.BlockSpec(memory_space=pl.ANY)] + [vmem] * 2,
        out_specs=(vmem, smem, vmem),
        scratch_shapes=[
            pltpu.VMEM((128, 128), F32),
            pltpu.VMEM((64, 128), F32),
            pltpu.VMEM((8, 160, 256), BF16),
            pltpu.VMEM((8, 16, 256), F32),
            pltpu.VMEM((8, 160, 256), BF16),
            pltpu.VMEM((8, 16, 256), F32),
            pltpu.VMEM((8, 160, 256), BF16),
            pltpu.VMEM((8, 16, 256), F32),
            pltpu.VMEM((7, 176, 256), BF16),
            pltpu.VMEM((7, 2, 128), F32),
            pltpu.VMEM((8, 176, 256), BF16),
            pltpu.VMEM((8, 2, 128), F32),
            pltpu.VMEM((176, 256), BF16),
            pltpu.VMEM((2, 128), F32),
            pltpu.VMEM((64, 256), BF16),
            pltpu.VMEM((128, 256), F32),
            pltpu.VMEM((128, 256), F32),
            pltpu.VMEM((128, 128), F32),
            pltpu.VMEM((16, 8, 128), F32),
            pltpu.VMEM((16, 128), BF16),
            pltpu.VMEM((16, 16, 128), BF16),
            pltpu.VMEM((16, 8, 256), BF16),
            pltpu.VMEM((16, 8, 256), BF16),
            pltpu.VMEM((32, 4, 128), BF16),
            pltpu.VMEM((32, 4, 128), BF16),
            sem((8,)), sem((8,)), sem((8,)), sem((8,)), sem((7,)), sem((7,)),
            sem((7,)), sem((7,)), sem((2,)), sem((2,)),
            sem((16,)), sem((16,)), sem((16,)), sem((16,)), sem((16,)), sem((16,)),
            sem((32,)), sem((32,)), sem(()),
            pltpu.SemaphoreType.REGULAR, pltpu.SemaphoreType.REGULAR,
        ],
        compiler_params=pltpu.CompilerParams(collective_id=0, has_side_effects=True),
        name="list",
    )(
        skip_gain, token_input[0], input_map[0], output_map[0], step_size[0].T, forget[0].T,
        segments[0], comparator.T, yield_rank, pair_mask[0],
    )
    return (loss, pooled_grad.astype(F32)[None], weight_grad)


def solution(mesh):
    return jax.shard_map(
        per_device,
        mesh=mesh,
        in_specs=(
            P("dp", "seq", None),
            P("dp", "seq", None),
            P("dp", "seq", None),
            P("dp", "seq", None),
            P("dp", "seq", None),
            P(),
            P("dp", "seq", None),
            P("dp", None),
            P("dp", "seq", None),
            P(),
        ),
        out_specs=(P("dp"), P("dp", "seq", None), P(("dp", "seq"), None)),
        check_vma=False,
    )
```

```python
import jax
import jax.numpy as jnp
from jax import lax
from jax.experimental import pallas as pl
from jax.experimental.pallas import tpu as pltpu
from jax.sharding import PartitionSpec as P

HI = lax.Precision.HIGHEST
F32 = jnp.float32
BF16 = jnp.bfloat16
EPS = 1e-05
NS = 16
ND = 32
COLS = 4
CHIPS = 8
AHEAD = 2
MESH = pl.DeviceIdType.MESH


def dot(a, b, precision=None):
    return lax.dot_general(
        a, b, (((1,), (0,)), ((), ())), precision=precision, preferred_element_type=F32
    )


def dot_t(a, b):
    return lax.dot_general(a, b, (((1,), (1,)), ((), ())), preferred_element_type=F32)


def iota(shape, axis):
    return lax.broadcasted_iota(jnp.int32, shape, axis)


def list_kernel(
    skip, tok, b_in, c_out, step, forget, seg, w_in, rank, mask,
    pg_o, loss_o, wg_o,
    cols, dl_rows, give_s, give_q, give_m, give_d, own_s, own_q, own_m, own_d,
    got_s, got_q, got_m, got_d, pack, pack_d,
    r_pack, r_dec, relay, relay_d, w_own,
    carried, means, margin_part, r_margin, pair_own, r_pair, grad_part, r_grad, w_part, r_w,
    send_g, recv_g, send_a, recv_a, send_ad, recv_ad, hop_s, hop_r, send_b, recv_b, send_c, recv_c,
    send_d, recv_d, send_w, recv_w, w_sem, line_sem, plane_sem,
):
    me_d = lax.axis_index("dp")
    me = lax.axis_index("seq")
    chip = me // 2
    core = lax.rem(me, 2)
    home = me_d // 2

    def peer(k):
        return lax.rem(me + k, NS)

    barrier = pltpu.get_barrier_semaphore()

    def greet(k, _):
        pl.semaphore_signal(barrier, inc=1, device_id=(me_d, peer(k)), device_id_type=MESH)
        return 0

    lax.fori_loop(1, NS, greet, 0)
    rows_y, cols_x = ND // COLS, COLS
    at_y, at_x = me_d // COLS, lax.rem(me_d, COLS)
    for k in range(1, rows_y):
        there = lax.rem(at_y + k, rows_y) * COLS + at_x
        pl.semaphore_signal(barrier, inc=1, device_id=(there, me), device_id_type=MESH)
    beside = [(at_y * COLS + lax.rem(at_x + k, cols_x), me) for k in range(1, cols_x)]
    for there in beside:
        pl.semaphore_signal(barrier, inc=1, device_id=there, device_id_type=MESH)
    w_fetch = pltpu.make_async_copy(
        w_in.at[:, pl.ds(pl.multiple_of(me * 256, 256), 256)], w_own, w_sem
    )
    w_fetch.start()

    upper = iota((128, 128), 0) <= iota((128, 128), 1)
    lower = iota((128, 128), 0) >= iota((128, 128), 1)
    dl = -dot(forget[...], upper.astype(F32), HI)
    end_weight = jnp.exp(dl[:, 127:128] - dl) * step[...]
    dl_rows[...] = dl
    cols[...] = jnp.transpose(jnp.concatenate([dl, end_weight], axis=0))
    b_t = jnp.transpose(b_in[...].astype(F32)).astype(BF16)
    scores = jnp.where(lower, dot_t(c_out[...], b_in[...]), 0.0)
    member = (jnp.broadcast_to(seg[...], (8, 128)) == iota((8, 128), 0)).astype(F32)
    member_low = member.astype(BF16)
    inverse = 1.0 / jnp.sum(member, axis=1, keepdims=True)
    average = member * inverse
    left = iota((128, 128), 1) < 64
    left8 = left[:8]

    gives = (give_s, give_q, give_m, give_d)
    owns = (own_s, own_q, own_m, own_d)
    gots = (got_s, got_q, got_m, got_d)

    def group(j, outs, t):
        out_s, out_q, out_m, out_d = outs
        here = pltpu.roll(cols[...], lax.rem(128 - 4 * j, 128), 1)
        query_rows = []
        for pair in range(2):
            lanes = pl.ds(pl.multiple_of(j * 256 + pair * 128, 128), 128)
            at_lanes = slice(pair * 128, pair * 128 + 128)
            tokens = tok[:, lanes]
            mixed = []
            totals = []
            for i in range(2):
                at = pair * 2 + i
                row = dl_rows[pl.ds(j * 4 + at, 1), :]
                gap = here[:, at : at + 1] - row
                mixing = scores * jnp.exp(jnp.minimum(gap, 0.0)) * step[pl.ds(j * 4 + at, 1), :]
                mixed.append(dot(member_low, mixing.astype(BF16)) + skip[j * 4 + at] * member)
                past = jnp.exp(row)
                query_rows.append(average * past)
                totals.append(past[:, 127:128])
            both = dot(jnp.concatenate(mixed, axis=0).astype(BF16), tokens)
            out_m[t, :, at_lanes] = jnp.where(left8, both[:8], both[8:]) * inverse
            out_d[t, pair : pair + 1, :] = jnp.where(left8[:1], totals[0], totals[1])
            base = 64 + pair * 2
            weight = jnp.where(left, here[:, base : base + 1], here[:, base + 1 : base + 2])
            scaled = (tokens.astype(F32) * weight).astype(BF16)
            out_s[t, :, at_lanes] = dot(b_t, scaled).astype(BF16)
        queries = dot(jnp.concatenate(query_rows, axis=0).astype(BF16), c_out[...])
        out_q[t] = queries.astype(BF16)

    def target_chip(t):
        away = CHIPS // 2 + (t // 2 + lax.rem(t, 2)) * (1 - 2 * lax.rem(t, 2))
        return lax.rem(chip + away, CHIPS)

    def compute(t, _):
        to = target_chip(t) * 2
        group(to + 1 - core, gives, t)
        group(to + core, owns, t)
        return 0

    def give(t):
        other = (me_d, chip * 2 + 1 - core)
        return [
            pltpu.make_async_remote_copy(
                src_ref=src.at[t], dst_ref=dst.at[t], send_sem=send_g.at[n, t],
                recv_sem=recv_g.at[n, t], device_id=other, device_id_type=MESH,
            )
            for n, (src, dst) in enumerate(zip(gives, gots))
        ]

    def send_give(t, _):
        for c in give(t):
            c.start()
        return 0

    lane = iota((8, 256), 1) // 64

    def by_head(rows):
        total = jnp.where(lane == 0, rows[0:8], 0.0)
        for h in range(1, 4):
            total = total + jnp.where(lane == h, rows[h * 8 : h * 8 + 8], 0.0)
        return total

    def combine(t, out, out_d, at):
        for c in give(t):
            c.wait()
        first = core == 0

        def ordered(n):
            mine, theirs = owns[n][t], gots[n][t]
            return jnp.where(first, mine, theirs), jnp.where(first, theirs, mine)

        early, late = ordered(0)
        early_q, late_q = ordered(1)
        early_m, late_m = ordered(2)
        early_2, late_2 = ordered(3)
        early_d = jnp.concatenate([early_2[0:1], early_2[1:2]], axis=1)
        late_d = jnp.concatenate([late_2[0:1], late_2[1:2]], axis=1)
        state = late_d * early.astype(F32) + late.astype(F32)
        within = by_head(dot(late_q, early))
        scaled_q = late_q.astype(F32)
        scaled_q = jnp.concatenate(
            [scaled_q[h * 8 : h * 8 + 8] * early_d[:, h * 64 : h * 64 + 1] for h in range(4)],
            axis=0,
        )
        out[at, 0:128, :] = state.astype(BF16)
        out[at, 128:160, 0:128] = early_q
        out[at, 128:160, 128:256] = scaled_q.astype(BF16)
        out[at, 160:176, :] = jnp.concatenate(
            [early_m, late_m + within], axis=0
        ).astype(BF16)
        out_d[at] = early_2 * late_2

    def package(t):
        to = (me_d, target_chip(t) * 2 + core)
        return (
            pltpu.make_async_remote_copy(
                src_ref=pack.at[t], dst_ref=r_pack.at[chip], send_sem=send_a.at[t],
                recv_sem=recv_a.at[t], device_id=to, device_id_type=MESH,
            ),
            pltpu.make_async_remote_copy(
                src_ref=pack_d.at[t], dst_ref=r_dec.at[chip], send_sem=send_ad.at[t],
                recv_sem=recv_ad.at[t], device_id=to, device_id_type=MESH,
            ),
        )

    way = 1 - 2 * core

    def chip_at(away):
        return lax.rem(chip + away * way + CHIPS, CHIPS)

    hop_to = (me_d, chip_at(1) * 2 + core)
    to_relay = (
        pltpu.make_async_remote_copy(
            src_ref=pack.at[0], dst_ref=relay, send_sem=hop_s.at[0], recv_sem=hop_r.at[0],
            device_id=hop_to, device_id_type=MESH,
        ),
        pltpu.make_async_remote_copy(
            src_ref=pack_d.at[0], dst_ref=relay_d, send_sem=hop_s.at[1], recv_sem=hop_r.at[1],
            device_id=hop_to, device_id_type=MESH,
        ),
    )
    end_at = (me_d, chip_at(3) * 2 + core)
    origin = chip_at(-1)
    forward = (
        pltpu.make_async_remote_copy(
            src_ref=relay, dst_ref=r_pack.at[origin], send_sem=send_a.at[0],
            recv_sem=recv_a.at[0], device_id=end_at, device_id_type=MESH,
        ),
        pltpu.make_async_remote_copy(
            src_ref=relay_d, dst_ref=r_dec.at[origin], send_sem=send_ad.at[0],
            recv_sem=recv_ad.at[0], device_id=end_at, device_id_type=MESH,
        ),
    )

    def send_package(t):
        @pl.when(t == 0)
        def _():
            for c in to_relay:
                c.start()

        @pl.when(t > 0)
        def _():
            for c in package(t):
                c.start()

    lax.fori_loop(0, AHEAD, compute, 0)
    pl.semaphore_wait(barrier, NS - 1 + rows_y - 1 + cols_x - 1)
    for there in beside:
        pl.semaphore_signal(line_sem, inc=1, device_id=there, device_id_type=MESH)
    lax.fori_loop(0, AHEAD, send_give, 0)

    def middle(t, _):
        combine(t - AHEAD, pack, pack_d, t - AHEAD)
        compute(t, 0)
        send_package(t - AHEAD)
        send_give(t, 0)
        return 0

    lax.fori_loop(AHEAD, CHIPS, middle, 0)
    combine(CHIPS - AHEAD, pack, pack_d, CHIPS - AHEAD)
    for c in to_relay:
        c.wait_recv()
    for c in forward:
        c.start()

    def rest(t, _):
        combine(t, pack, pack_d, t)
        send_package(t - 1)
        return 0

    lax.fori_loop(CHIPS - AHEAD + 1, CHIPS - 1, rest, 0)
    combine(CHIPS - 1, r_pack, r_dec, chip)
    for c in package(CHIPS - 2):
        c.start()

    pl.semaphore_wait(line_sem, cols_x - 1)

    def tell(k, _):
        pl.semaphore_signal(plane_sem, inc=1, device_id=(me_d, peer(k)), device_id_type=MESH)
        return 0

    lax.fori_loop(1, NS, tell, 0)
    w_fetch.wait()
    narrow = w_own[...].astype(F32)
    same = (iota((256, 256), 0) // 64) == (iota((256, 256), 1) // 64)
    blocks_t = jnp.where(same, jnp.concatenate([narrow, narrow, narrow, narrow], axis=0), 0.0)
    blocks = jnp.transpose(blocks_t)
    weight = blocks.astype(BF16)
    skewed = (blocks_t - blocks).astype(BF16)
    spread = jnp.where(same, 1.0 / 64.0, 0.0).astype(BF16)
    carried[...] = jnp.zeros_like(carried)

    def chip_step(b, _):
        away = lax.rem(chip - b + CHIPS, CHIPS)
        half = CHIPS // 2
        order = jnp.where(away < half, CHIPS - 1 - 2 * away, 2 * (away - half))

        @pl.when(b != chip)
        def _():
            for c in package(order):
                c.wait_recv()

        now = carried[...]
        queries = jnp.concatenate([r_pack[b, 128:160, 0:128], r_pack[b, 128:160, 128:256]], axis=0)
        past = dot(queries, now.astype(BF16))
        local = r_pack[b, 160:176, :].astype(F32)
        means[pl.ds(pl.multiple_of(b * 16, 16), 16), :] = local + jnp.concatenate(
            [by_head(past[:32]), by_head(past[32:])], axis=0
        )
        decay = jnp.concatenate([r_dec[b, 0:1, :], r_dec[b, 1:2, :]], axis=1)
        carried[...] = decay * now + r_pack[b, 0:128, :].astype(F32)
        return 0

    lax.fori_loop(0, CHIPS, chip_step, 0)

    def exchange(src, dst, send, recv, k):
        return pltpu.make_async_remote_copy(
            src_ref=src, dst_ref=dst, send_sem=send, recv_sem=recv,
            device_id=(me_d, peer(k)), device_id_type=MESH,
        )

    mean = means[...]
    squared = mean * mean
    squared_high = squared.astype(BF16)
    squared_low = (squared - squared_high.astype(F32)).astype(BF16)
    square = dot(squared_high, spread) + dot(squared_low, spread)
    pooled = (mean * lax.rsqrt(square + EPS)).astype(BF16)
    projected = dot(pooled, weight).astype(BF16)
    margin_part[...] = dot_t(projected, pooled) - dot_t(pooled, projected)

    def margin_copy(k):
        rows = pl.ds(pl.multiple_of(peer(k) * 8, 8), 8)
        return exchange(margin_part.at[rows], r_margin.at[k], send_b.at[k], recv_b.at[k], k)

    def start_b(k, _):
        margin_copy(k).start()
        return 0

    lax.fori_loop(1, NS, start_b, 0, unroll=True)
    r_margin[0] = margin_part[pl.ds(pl.multiple_of(me * 8, 8), 8), :]
    skew_rows = dot(pooled, skewed).astype(BF16)
    pooled_t = jnp.transpose(pooled.astype(F32)).astype(BF16)
    ranks = jnp.broadcast_to(rank[...].astype(F32), (8, 128))
    mine = iota((8, 128), 1) == me * 8 + iota((8, 128), 0)
    own_rank = jnp.sum(jnp.where(mine, ranks, 0.0), axis=1, keepdims=True)
    target = jnp.where(own_rank < ranks, 1.0, jnp.where(own_rank > ranks, 0.0, 0.5))
    valid = mask[...].astype(F32)

    def wait_b(k, _):
        margin_copy(k).wait()
        return 0

    lax.fori_loop(1, NS, wait_b, 0)
    margin = jnp.sum(r_margin[...], axis=0)
    soft = jnp.maximum(margin, 0.0) + jnp.log(1.0 + jnp.exp(-jnp.abs(margin)))
    losses = jnp.sum(valid * (soft - target * margin), axis=0, keepdims=True)
    pair = 2.0 * valid * (1.0 / (1.0 + jnp.exp(-margin)) - target)
    loss_high = losses.astype(BF16).astype(F32)
    loss_rows = jnp.where(iota((8, 128), 0) == 0, loss_high, losses - loss_high)
    sent = jnp.concatenate([pair, loss_rows], axis=0).astype(BF16)
    pair_own[...] = sent
    r_pair[me] = sent

    def pair_copy(k):
        return exchange(pair_own, r_pair.at[me], send_c.at[k], recv_c.at[k], k)

    def start_c(k, _):
        pair_copy(k).start()
        return 0

    lax.fori_loop(1, NS, start_c, 0, unroll=True)

    pl.semaphore_wait(plane_sem, NS - 1)

    def wait_c(k, _):
        pair_copy(k).wait()
        return 0

    lax.fori_loop(1, NS, wait_c, 0)
    pairs = r_pair[...].astype(F32)
    all_pair = pairs[:, :8, :].reshape(128, 128).astype(BF16)
    accumulated = dot(all_pair, pooled)
    high = accumulated.astype(BF16)
    low = (accumulated - high.astype(F32)).astype(BF16)
    product = (dot(pooled_t, high) + dot(pooled_t, low)) * (1.0 / 4096.0)
    for i in range(2 * NS):
        h = i // 8
        piece = product[i * 8 : i * 8 + 8, h * 64 : h * 64 + 64]
        w_part[i] = jnp.concatenate([piece[:4], piece[4:]], axis=1).astype(BF16)

    def w_copy(i):
        to_d = me * 2 + i // NS
        to_s = lax.rem(i, NS)
        return to_d, to_s, pltpu.make_async_remote_copy(
            src_ref=w_part.at[i],
            dst_ref=r_w.at[me_d],
            send_sem=send_w.at[i], recv_sem=recv_w.at[me_d],
            device_id=(to_d, to_s), device_id_type=MESH,
        )

    def start_w(i, _):
        to_d, to_s, c = w_copy(i)
        itself = jnp.logical_and(to_d == me_d, to_s == me)

        @pl.when(jnp.logical_not(itself))
        def _():
            c.start()

        @pl.when(itself)
        def _():
            r_w[me_d] = w_part[i]

        return 0

    lax.fori_loop(0, 2 * NS, start_w, 0, unroll=4)
    grad_part[...] = dot(all_pair, skew_rows).astype(BF16).reshape(NS, 8, 256)

    def grad_copy(k):
        return exchange(grad_part.at[peer(k)], r_grad.at[me], send_d.at[k], recv_d.at[k], k)

    def start_d(k, _):
        grad_copy(k).start()
        return 0

    lax.fori_loop(1, NS, start_d, 0, unroll=True)
    r_grad[me] = grad_part[me]
    loss_o[0] = jnp.sum(pairs[:, 8:10, :]) * (1.0 / (128.0 * 128.0))

    for c in to_relay:
        c.wait_send()

    def wait_a(t, _):
        for c in package(t):
            c.wait_send()
        return 0

    lax.fori_loop(0, CHIPS - 1, wait_a, 0)

    def wait_d(k, _):
        grad_copy(k).wait()
        return 0

    lax.fori_loop(1, NS, wait_d, 0)
    for b in range(NS):
        pg_o[:, b * 256 : b * 256 + 256] = r_grad[b]

    def wait_w(i, _):
        to_d, to_s, c = w_copy(i)

        @pl.when(jnp.logical_not(jnp.logical_and(to_d == me_d, to_s == me)))
        def _():
            c.wait_send()

        arrived = pltpu.make_async_remote_copy(
            src_ref=w_part.at[0], dst_ref=r_w.at[i],
            send_sem=send_w.at[i], recv_sem=recv_w.at[i],
            device_id=(to_d, to_s), device_id_type=MESH,
        )

        @pl.when(jnp.logical_or(i != me_d, home != me))
        def _():
            arrived.wait_recv()

        return 0

    lax.fori_loop(0, ND, wait_w, 0)
    folded = jnp.sum(r_w[...].astype(F32), axis=0)
    wg_o[...] = jnp.concatenate([folded[:, :64], folded[:, 64:]], axis=0)


def per_device(
    token_input, input_map, output_map, step_size, forget, skip_gain, segments, yield_rank,
    pair_mask, comparator,
):
    vmem = pl.BlockSpec(memory_space=pltpu.VMEM)
    smem = pl.BlockSpec(memory_space=pltpu.SMEM)
    shape = jax.ShapeDtypeStruct
    sem = pltpu.SemaphoreType.DMA
    pooled_grad, loss, weight_grad = pl.pallas_call(
        list_kernel,
        out_shape=(shape((8, 4096), BF16), shape((1,), F32), shape((8, 64), F32)),
        in_specs=[smem] + [vmem] * 6 + [pl.BlockSpec(memory_space=pl.ANY)] + [vmem] * 2,
        out_specs=(vmem, smem, vmem),
        scratch_shapes=[
            pltpu.VMEM((128, 128), F32),
            pltpu.VMEM((64, 128), F32),
            pltpu.VMEM((8, 128, 256), BF16),
            pltpu.VMEM((8, 32, 128), BF16),
            pltpu.VMEM((8, 8, 256), F32),
            pltpu.VMEM((8, 2, 128), F32),
            pltpu.VMEM((8, 128, 256), BF16),
            pltpu.VMEM((8, 32, 128), BF16),
            pltpu.VMEM((8, 8, 256), F32),
            pltpu.VMEM((8, 2, 128), F32),
            pltpu.VMEM((8, 128, 256), BF16),
            pltpu.VMEM((8, 32, 128), BF16),
            pltpu.VMEM((8, 8, 256), F32),
            pltpu.VMEM((8, 2, 128), F32),
            pltpu.VMEM((7, 176, 256), BF16),
            pltpu.VMEM((7, 2, 128), F32),
            pltpu.VMEM((8, 176, 256), BF16),
            pltpu.VMEM((8, 2, 128), F32),
            pltpu.VMEM((176, 256), BF16),
            pltpu.VMEM((2, 128), F32),
            pltpu.VMEM((64, 256), BF16),
            pltpu.VMEM((128, 256), F32),
            pltpu.VMEM((128, 256), F32),
            pltpu.VMEM((128, 128), F32),
            pltpu.VMEM((16, 8, 128), F32),
            pltpu.VMEM((16, 128), BF16),
            pltpu.VMEM((16, 16, 128), BF16),
            pltpu.VMEM((16, 8, 256), BF16),
            pltpu.VMEM((16, 8, 256), BF16),
            pltpu.VMEM((32, 4, 128), BF16),
            pltpu.VMEM((32, 4, 128), BF16),
            sem((4, 8)), sem((4, 8)), sem((7,)), sem((7,)),
            sem((7,)), sem((7,)), sem((2,)), sem((2,)),
            sem((16,)), sem((16,)), sem((16,)), sem((16,)), sem((16,)), sem((16,)),
            sem((32,)), sem((32,)), sem(()),
            pltpu.SemaphoreType.REGULAR, pltpu.SemaphoreType.REGULAR,
        ],
        compiler_params=pltpu.CompilerParams(collective_id=0, has_side_effects=True),
        name="list",
    )(
        skip_gain, token_input[0], input_map[0], output_map[0], step_size[0].T, forget[0].T,
        segments[0], comparator.T, yield_rank, pair_mask[0],
    )
    return (loss, pooled_grad.astype(F32)[None], weight_grad)


def solution(mesh):
    return jax.shard_map(
        per_device,
        mesh=mesh,
        in_specs=(
            P("dp", "seq", None),
            P("dp", "seq", None),
            P("dp", "seq", None),
            P("dp", "seq", None),
            P("dp", "seq", None),
            P(),
            P("dp", "seq", None),
            P("dp", None),
            P("dp", "seq", None),
            P(),
        ),
        out_specs=(P("dp"), P("dp", "seq", None), P(("dp", "seq"), None)),
        check_vma=False,
    )
```

```python
import jax
import jax.numpy as jnp
from jax import lax
from jax.experimental import pallas as pl
from jax.experimental.pallas import tpu as pltpu
from jax.sharding import PartitionSpec as P

HI = lax.Precision.HIGHEST
F32 = jnp.float32
BF16 = jnp.bfloat16
EPS = 1e-05
NS = 16
ND = 32
COLS = 4
CHIPS = 8
AHEAD = 2
MESH = pl.DeviceIdType.MESH
NEAR_FIRST = sorted(range(1, NS), key=lambda k: min(k, NS - k))


def dot(a, b, precision=None):
    return lax.dot_general(
        a, b, (((1,), (0,)), ((), ())), precision=precision, preferred_element_type=F32
    )


def dot_t(a, b):
    return lax.dot_general(a, b, (((1,), (1,)), ((), ())), preferred_element_type=F32)


def iota(shape, axis):
    return lax.broadcasted_iota(jnp.int32, shape, axis)


def list_kernel(
    skip, tok, b_in, c_out, step, forget, seg, w_in, rank, mask,
    pg_o, loss_o, wg_o,
    cols, dl_rows, give_s, give_q, give_m, give_d, own_s, own_q, own_m, own_d,
    got_s, got_q, got_m, got_d, pack, pack_d,
    r_pack, r_dec, relay, relay_d, w_own,
    carried, means, margin_part, r_margin, pair_own, r_pair, grad_part, r_grad, w_part, r_w,
    send_g, recv_g, send_a, recv_a, send_ad, recv_ad, hop_s, hop_r, send_b, recv_b, send_c, recv_c,
    send_d, recv_d, send_w, recv_w, w_sem, line_sem, plane_sem,
):
    me_d = lax.axis_index("dp")
    me = lax.axis_index("seq")
    chip = me // 2
    core = lax.rem(me, 2)
    home = me_d // 2

    def peer(k):
        return lax.rem(me + k, NS)

    barrier = pltpu.get_barrier_semaphore()

    def greet(k, _):
        pl.semaphore_signal(barrier, inc=1, device_id=(me_d, peer(k)), device_id_type=MESH)
        return 0

    lax.fori_loop(1, NS, greet, 0)
    rows_y, cols_x = ND // COLS, COLS
    at_y, at_x = me_d // COLS, lax.rem(me_d, COLS)
    for k in range(1, rows_y):
        there = lax.rem(at_y + k, rows_y) * COLS + at_x
        pl.semaphore_signal(barrier, inc=1, device_id=(there, me), device_id_type=MESH)
    beside = [(at_y * COLS + lax.rem(at_x + k, cols_x), me) for k in range(1, cols_x)]
    for there in beside:
        pl.semaphore_signal(barrier, inc=1, device_id=there, device_id_type=MESH)
    w_fetch = pltpu.make_async_copy(
        w_in.at[:, pl.ds(pl.multiple_of(me * 256, 256), 256)], w_own, w_sem
    )
    w_fetch.start()

    upper = iota((128, 128), 0) <= iota((128, 128), 1)
    lower = iota((128, 128), 0) >= iota((128, 128), 1)
    dl = -dot(forget[...], upper.astype(F32), HI)
    end_weight = jnp.exp(dl[:, 127:128] - dl) * step[...]
    dl_rows[...] = dl
    cols[...] = jnp.transpose(jnp.concatenate([dl, end_weight], axis=0))
    b_t = jnp.transpose(b_in[...].astype(F32)).astype(BF16)
    scores = jnp.where(lower, dot_t(c_out[...], b_in[...]), 0.0)
    member = (jnp.broadcast_to(seg[...], (8, 128)) == iota((8, 128), 0)).astype(F32)
    member_low = member.astype(BF16)
    inverse = 1.0 / jnp.sum(member, axis=1, keepdims=True)
    average = member * inverse
    left = iota((128, 128), 1) < 64
    left8 = left[:8]

    gives = (give_s, give_q, give_m, give_d)
    owns = (own_s, own_q, own_m, own_d)
    gots = (got_s, got_q, got_m, got_d)

    def group(j, outs, t):
        out_s, out_q, out_m, out_d = outs
        here = pltpu.roll(cols[...], lax.rem(128 - 4 * j, 128), 1)
        query_rows = []
        for pair in range(2):
            lanes = pl.ds(pl.multiple_of(j * 256 + pair * 128, 128), 128)
            at_lanes = slice(pair * 128, pair * 128 + 128)
            tokens = tok[:, lanes]
            mixed = []
            totals = []
            for i in range(2):
                at = pair * 2 + i
                row = dl_rows[pl.ds(j * 4 + at, 1), :]
                gap = here[:, at : at + 1] - row
                mixing = scores * jnp.exp(jnp.minimum(gap, 0.0)) * step[pl.ds(j * 4 + at, 1), :]
                mixed.append(dot(member_low, mixing.astype(BF16)) + skip[j * 4 + at] * member)
                past = jnp.exp(row)
                query_rows.append(average * past)
                totals.append(past[:, 127:128])
            both = dot(jnp.concatenate(mixed, axis=0).astype(BF16), tokens)
            out_m[t, :, at_lanes] = jnp.where(left8, both[:8], both[8:]) * inverse
            out_d[t, pair : pair + 1, :] = jnp.where(left8[:1], totals[0], totals[1])
            base = 64 + pair * 2
            weight = jnp.where(left, here[:, base : base + 1], here[:, base + 1 : base + 2])
            scaled = (tokens.astype(F32) * weight).astype(BF16)
            out_s[t, :, at_lanes] = dot(b_t, scaled).astype(BF16)
        queries = dot(jnp.concatenate(query_rows, axis=0).astype(BF16), c_out[...])
        out_q[t] = queries.astype(BF16)

    def target_chip(t):
        away = CHIPS // 2 + (t // 2 + lax.rem(t, 2)) * (1 - 2 * lax.rem(t, 2))
        return lax.rem(chip + away, CHIPS)

    def compute(t, _):
        to = target_chip(t) * 2
        group(to + 1 - core, gives, t)
        group(to + core, owns, t)
        return 0

    def give(t):
        other = (me_d, chip * 2 + 1 - core)
        return [
            pltpu.make_async_remote_copy(
                src_ref=src.at[t], dst_ref=dst.at[t], send_sem=send_g.at[n, t],
                recv_sem=recv_g.at[n, t], device_id=other, device_id_type=MESH,
            )
            for n, (src, dst) in enumerate(zip(gives, gots))
        ]

    def send_give(t, _):
        for c in give(t):
            c.start()
        return 0

    lane = iota((8, 256), 1) // 64

    def by_head(rows):
        total = jnp.where(lane == 0, rows[0:8], 0.0)
        for h in range(1, 4):
            total = total + jnp.where(lane == h, rows[h * 8 : h * 8 + 8], 0.0)
        return total

    def combine(t, out, out_d, at):
        for c in give(t):
            c.wait()
        first = core == 0

        def ordered(n):
            mine, theirs = owns[n][t], gots[n][t]
            return jnp.where(first, mine, theirs), jnp.where(first, theirs, mine)

        early, late = ordered(0)
        early_q, late_q = ordered(1)
        early_m, late_m = ordered(2)
        early_2, late_2 = ordered(3)
        early_d = jnp.concatenate([early_2[0:1], early_2[1:2]], axis=1)
        late_d = jnp.concatenate([late_2[0:1], late_2[1:2]], axis=1)
        state = late_d * early.astype(F32) + late.astype(F32)
        within = by_head(dot(late_q, early))
        scaled_q = late_q.astype(F32)
        scaled_q = jnp.concatenate(
            [scaled_q[h * 8 : h * 8 + 8] * early_d[:, h * 64 : h * 64 + 1] for h in range(4)],
            axis=0,
        )
        out[at, 0:128, :] = state.astype(BF16)
        out[at, 128:160, 0:128] = early_q
        out[at, 128:160, 128:256] = scaled_q.astype(BF16)
        out[at, 160:176, :] = jnp.concatenate(
            [early_m, late_m + within], axis=0
        ).astype(BF16)
        out_d[at] = early_2 * late_2

    def package(t):
        to = (me_d, target_chip(t) * 2 + core)
        return (
            pltpu.make_async_remote_copy(
                src_ref=pack.at[t], dst_ref=r_pack.at[chip], send_sem=send_a.at[t],
                recv_sem=recv_a.at[t], device_id=to, device_id_type=MESH,
            ),
            pltpu.make_async_remote_copy(
                src_ref=pack_d.at[t], dst_ref=r_dec.at[chip], send_sem=send_ad.at[t],
                recv_sem=recv_ad.at[t], device_id=to, device_id_type=MESH,
            ),
        )

    way = 1 - 2 * core

    def chip_at(away):
        return lax.rem(chip + away * way + CHIPS, CHIPS)

    hop_to = (me_d, chip_at(1) * 2 + core)
    to_relay = (
        pltpu.make_async_remote_copy(
            src_ref=pack.at[0], dst_ref=relay, send_sem=hop_s.at[0], recv_sem=hop_r.at[0],
            device_id=hop_to, device_id_type=MESH,
        ),
        pltpu.make_async_remote_copy(
            src_ref=pack_d.at[0], dst_ref=relay_d, send_sem=hop_s.at[1], recv_sem=hop_r.at[1],
            device_id=hop_to, device_id_type=MESH,
        ),
    )
    end_at = (me_d, chip_at(3) * 2 + core)
    origin = chip_at(-1)
    forward = (
        pltpu.make_async_remote_copy(
            src_ref=relay, dst_ref=r_pack.at[origin], send_sem=send_a.at[0],
            recv_sem=recv_a.at[0], device_id=end_at, device_id_type=MESH,
        ),
        pltpu.make_async_remote_copy(
            src_ref=relay_d, dst_ref=r_dec.at[origin], send_sem=send_ad.at[0],
            recv_sem=recv_ad.at[0], device_id=end_at, device_id_type=MESH,
        ),
    )

    def send_package(t):
        @pl.when(t == 0)
        def _():
            for c in to_relay:
                c.start()

        @pl.when(t > 0)
        def _():
            for c in package(t):
                c.start()

    lax.fori_loop(0, AHEAD, compute, 0)
    pl.semaphore_wait(barrier, NS - 1 + rows_y - 1 + cols_x - 1)
    for there in beside:
        pl.semaphore_signal(line_sem, inc=1, device_id=there, device_id_type=MESH)
    lax.fori_loop(0, AHEAD, send_give, 0)

    def middle(t, _):
        combine(t - AHEAD, pack, pack_d, t - AHEAD)
        compute(t, 0)
        send_package(t - AHEAD)
        send_give(t, 0)
        return 0

    lax.fori_loop(AHEAD, CHIPS, middle, 0)
    combine(CHIPS - AHEAD, pack, pack_d, CHIPS - AHEAD)
    for c in to_relay:
        c.wait_recv()
    for c in forward:
        c.start()

    def rest(t, _):
        combine(t, pack, pack_d, t)
        send_package(t - 1)
        return 0

    lax.fori_loop(CHIPS - AHEAD + 1, CHIPS - 1, rest, 0)
    combine(CHIPS - 1, r_pack, r_dec, chip)
    for c in package(CHIPS - 2):
        c.start()

    pl.semaphore_wait(line_sem, cols_x - 1)

    def tell(k, _):
        pl.semaphore_signal(plane_sem, inc=1, device_id=(me_d, peer(k)), device_id_type=MESH)
        return 0

    lax.fori_loop(1, NS, tell, 0)
    w_fetch.wait()
    narrow = w_own[...].astype(F32)
    same = (iota((256, 256), 0) // 64) == (iota((256, 256), 1) // 64)
    blocks_t = jnp.where(same, jnp.concatenate([narrow, narrow, narrow, narrow], axis=0), 0.0)
    blocks = jnp.transpose(blocks_t)
    weight = blocks.astype(BF16)
    skewed = (blocks_t - blocks).astype(BF16)
    spread = jnp.where(same, 1.0 / 64.0, 0.0).astype(BF16)
    carried[...] = jnp.zeros_like(carried)

    def chip_step(b, _):
        away = lax.rem(chip - b + CHIPS, CHIPS)
        half = CHIPS // 2
        order = jnp.where(away < half, CHIPS - 1 - 2 * away, 2 * (away - half))

        @pl.when(b != chip)
        def _():
            for c in package(order):
                c.wait_recv()

        now = carried[...]
        queries = jnp.concatenate([r_pack[b, 128:160, 0:128], r_pack[b, 128:160, 128:256]], axis=0)
        past = dot(queries, now.astype(BF16))
        local = r_pack[b, 160:176, :].astype(F32)
        means[pl.ds(pl.multiple_of(b * 16, 16), 16), :] = local + jnp.concatenate(
            [by_head(past[:32]), by_head(past[32:])], axis=0
        )
        decay = jnp.concatenate([r_dec[b, 0:1, :], r_dec[b, 1:2, :]], axis=1)
        carried[...] = decay * now + r_pack[b, 0:128, :].astype(F32)
        return 0

    lax.fori_loop(0, CHIPS, chip_step, 0)

    def exchange(src, dst, send, recv, k):
        return pltpu.make_async_remote_copy(
            src_ref=src, dst_ref=dst, send_sem=send, recv_sem=recv,
            device_id=(me_d, peer(k)), device_id_type=MESH,
        )

    mean = means[...]
    squared = mean * mean
    squared_high = squared.astype(BF16)
    squared_low = (squared - squared_high.astype(F32)).astype(BF16)
    square = dot(squared_high, spread) + dot(squared_low, spread)
    pooled = (mean * lax.rsqrt(square + EPS)).astype(BF16)
    projected = dot(pooled, weight).astype(BF16)
    margin_part[...] = dot_t(projected, pooled) - dot_t(pooled, projected)

    def margin_copy(k):
        rows = pl.ds(pl.multiple_of(peer(k) * 8, 8), 8)
        return exchange(margin_part.at[rows], r_margin.at[k], send_b.at[k], recv_b.at[k], k)

    for k in reversed(NEAR_FIRST):
        margin_copy(k).start()
    r_margin[0] = margin_part[pl.ds(pl.multiple_of(me * 8, 8), 8), :]
    skew_rows = dot(pooled, skewed).astype(BF16)
    pooled_t = jnp.transpose(pooled.astype(F32)).astype(BF16)
    ranks = jnp.broadcast_to(rank[...].astype(F32), (8, 128))
    mine = iota((8, 128), 1) == me * 8 + iota((8, 128), 0)
    own_rank = jnp.sum(jnp.where(mine, ranks, 0.0), axis=1, keepdims=True)
    target = jnp.where(own_rank < ranks, 1.0, jnp.where(own_rank > ranks, 0.0, 0.5))
    valid = mask[...].astype(F32)

    for k in NEAR_FIRST:
        margin_copy(k).wait_recv()
    margin = jnp.sum(r_margin[...], axis=0)
    soft = jnp.maximum(margin, 0.0) + jnp.log(1.0 + jnp.exp(-jnp.abs(margin)))
    losses = jnp.sum(valid * (soft - target * margin), axis=0, keepdims=True)
    pair = 2.0 * valid * (1.0 / (1.0 + jnp.exp(-margin)) - target)
    loss_high = losses.astype(BF16).astype(F32)
    loss_rows = jnp.where(iota((8, 128), 0) == 0, loss_high, losses - loss_high)
    sent = jnp.concatenate([pair, loss_rows], axis=0).astype(BF16)
    pair_own[...] = sent
    r_pair[me] = sent

    def pair_copy(k):
        return exchange(pair_own, r_pair.at[me], send_c.at[k], recv_c.at[k], k)

    for k in reversed(NEAR_FIRST):
        pair_copy(k).start()

    pl.semaphore_wait(plane_sem, NS - 1)

    for k in NEAR_FIRST:
        pair_copy(k).wait_recv()
    pairs = r_pair[...].astype(F32)
    all_pair = pairs[:, :8, :].reshape(128, 128).astype(BF16)
    accumulated = dot(all_pair, pooled)
    high = accumulated.astype(BF16)
    low = (accumulated - high.astype(F32)).astype(BF16)
    product = (dot(pooled_t, high) + dot(pooled_t, low)) * (1.0 / 4096.0)
    for i in range(2 * NS):
        h = i // 8
        piece = product[i * 8 : i * 8 + 8, h * 64 : h * 64 + 64]
        w_part[i] = jnp.concatenate([piece[:4], piece[4:]], axis=1).astype(BF16)

    def w_copy(i):
        to_d = me * 2 + i // NS
        to_s = lax.rem(i, NS)
        return to_d, to_s, pltpu.make_async_remote_copy(
            src_ref=w_part.at[i],
            dst_ref=r_w.at[me_d],
            send_sem=send_w.at[i], recv_sem=recv_w.at[me_d],
            device_id=(to_d, to_s), device_id_type=MESH,
        )

    def start_w(i, _):
        to_d, to_s, c = w_copy(i)
        itself = jnp.logical_and(to_d == me_d, to_s == me)

        @pl.when(jnp.logical_not(itself))
        def _():
            c.start()

        @pl.when(itself)
        def _():
            r_w[me_d] = w_part[i]

        return 0

    lax.fori_loop(0, 2 * NS, start_w, 0, unroll=4)
    grad_part[...] = dot(all_pair, skew_rows).astype(BF16).reshape(NS, 8, 256)

    def grad_copy(k):
        return exchange(grad_part.at[peer(k)], r_grad.at[me], send_d.at[k], recv_d.at[k], k)

    for k in reversed(NEAR_FIRST):
        grad_copy(k).start()
    r_grad[me] = grad_part[me]
    loss_o[0] = jnp.sum(pairs[:, 8:10, :]) * (1.0 / (128.0 * 128.0))

    for c in to_relay:
        c.wait_send()

    def wait_a(t, _):
        for c in package(t):
            c.wait_send()
        return 0

    lax.fori_loop(0, CHIPS - 1, wait_a, 0)

    for k in NEAR_FIRST:
        grad_copy(k).wait_recv()
    for b in range(NS):
        pg_o[:, b * 256 : b * 256 + 256] = r_grad[b]

    def wait_sent(k, _):
        margin_copy(k).wait_send()
        pair_copy(k).wait_send()
        grad_copy(k).wait_send()
        return 0

    lax.fori_loop(1, NS, wait_sent, 0)

    def wait_w_sent(i, _):
        to_d, to_s, c = w_copy(i)

        @pl.when(jnp.logical_not(jnp.logical_and(to_d == me_d, to_s == me)))
        def _():
            c.wait_send()

        return 0

    lax.fori_loop(0, ND, wait_w_sent, 0)

    def wait_w(i, _):
        arrived = pltpu.make_async_remote_copy(
            src_ref=w_part.at[0], dst_ref=r_w.at[i],
            send_sem=send_w.at[i], recv_sem=recv_w.at[i],
            device_id=(me_d, peer(1)), device_id_type=MESH,
        )

        @pl.when(jnp.logical_or(i != me_d, home != me))
        def _():
            arrived.wait_recv()

        return 0

    lax.fori_loop(0, ND, wait_w, 0, unroll=4)
    folded = jnp.sum(r_w[...].astype(F32), axis=0)
    wg_o[...] = jnp.concatenate([folded[:, :64], folded[:, 64:]], axis=0)


def per_device(
    token_input, input_map, output_map, step_size, forget, skip_gain, segments, yield_rank,
    pair_mask, comparator,
):
    vmem = pl.BlockSpec(memory_space=pltpu.VMEM)
    smem = pl.BlockSpec(memory_space=pltpu.SMEM)
    shape = jax.ShapeDtypeStruct
    sem = pltpu.SemaphoreType.DMA
    pooled_grad, loss, weight_grad = pl.pallas_call(
        list_kernel,
        out_shape=(shape((8, 4096), BF16), shape((1,), F32), shape((8, 64), F32)),
        in_specs=[smem] + [vmem] * 6 + [pl.BlockSpec(memory_space=pl.ANY)] + [vmem] * 2,
        out_specs=(vmem, smem, vmem),
        scratch_shapes=[
            pltpu.VMEM((128, 128), F32),
            pltpu.VMEM((64, 128), F32),
            pltpu.VMEM((8, 128, 256), BF16),
            pltpu.VMEM((8, 32, 128), BF16),
            pltpu.VMEM((8, 8, 256), F32),
            pltpu.VMEM((8, 2, 128), F32),
            pltpu.VMEM((8, 128, 256), BF16),
            pltpu.VMEM((8, 32, 128), BF16),
            pltpu.VMEM((8, 8, 256), F32),
            pltpu.VMEM((8, 2, 128), F32),
            pltpu.VMEM((8, 128, 256), BF16),
            pltpu.VMEM((8, 32, 128), BF16),
            pltpu.VMEM((8, 8, 256), F32),
            pltpu.VMEM((8, 2, 128), F32),
            pltpu.VMEM((7, 176, 256), BF16),
            pltpu.VMEM((7, 2, 128), F32),
            pltpu.VMEM((8, 176, 256), BF16),
            pltpu.VMEM((8, 2, 128), F32),
            pltpu.VMEM((176, 256), BF16),
            pltpu.VMEM((2, 128), F32),
            pltpu.VMEM((64, 256), BF16),
            pltpu.VMEM((128, 256), F32),
            pltpu.VMEM((128, 256), F32),
            pltpu.VMEM((128, 128), F32),
            pltpu.VMEM((16, 8, 128), F32),
            pltpu.VMEM((16, 128), BF16),
            pltpu.VMEM((16, 16, 128), BF16),
            pltpu.VMEM((16, 8, 256), BF16),
            pltpu.VMEM((16, 8, 256), BF16),
            pltpu.VMEM((32, 4, 128), BF16),
            pltpu.VMEM((32, 4, 128), BF16),
            sem((4, 8)), sem((4, 8)), sem((7,)), sem((7,)),
            sem((7,)), sem((7,)), sem((2,)), sem((2,)),
            sem((16,)), sem((16,)), sem((16,)), sem((16,)), sem((16,)), sem((16,)),
            sem((32,)), sem((32,)), sem(()),
            pltpu.SemaphoreType.REGULAR, pltpu.SemaphoreType.REGULAR,
        ],
        compiler_params=pltpu.CompilerParams(collective_id=0, has_side_effects=True),
        name="list",
    )(
        skip_gain, token_input[0], input_map[0], output_map[0], step_size[0].T, forget[0].T,
        segments[0], comparator.T, yield_rank, pair_mask[0],
    )
    return (loss, pooled_grad.astype(F32)[None], weight_grad)


def solution(mesh):
    return jax.shard_map(
        per_device,
        mesh=mesh,
        in_specs=(
            P("dp", "seq", None),
            P("dp", "seq", None),
            P("dp", "seq", None),
            P("dp", "seq", None),
            P("dp", "seq", None),
            P(),
            P("dp", "seq", None),
            P("dp", None),
            P("dp", "seq", None),
            P(),
        ),
        out_specs=(P("dp"), P("dp", "seq", None), P(("dp", "seq"), None)),
        check_vma=False,
    )
```
